32 devices in a mesh: outer: 4 (over y, core), inner: 2 (over x), region: 4 (over z).
Axes of the slice: x: 2, y: 2, z: 4, core: 2. Of those that a mesh axis runs over, the one named last changes fastest.
Arguments:
- observations: float32 [64, 128], P(('region', 'outer', 'inner')), parts along dimension 0, may hold values from -6 to 6
- obs_mask: int32 [64, 128], P(('region', 'outer', 'inner')), parts along dimension 0, may hold values 0 or 1
- sensor_map: int32 [512], P('region'), parts along dimension 0, may hold values from 0 to 127
- transition: float32 [128, 128], replicated, may hold values from -1 to 1
- proc_noise: float32 [128, 128], replicated, may hold values from -1 to 1, as said below
- obs_var: float32 [128], replicated, may hold values from 0.1 to 1
- prior_mean: float32 [512], P('region'), parts along dimension 0, may hold values from -6 to 6
- prior_var: float32 [512], P('region'), parts along dimension 0, may hold values from 0.5 to 4
Outputs:
- filt_mean: float32 [64, 128], P(('region', 'outer', 'inner')), parts along dimension 0
- filt_cov: float32 [64, 128, 128], P(('region', 'outer', 'inner')), parts along dimension 0
The draws below stay inside these ranges and needn't reach their ends.
There are 4 independent parts, one for each index of `region`. The reference program is written for one: setup_inputs(seed, part) draws one part's arguments, and reference() takes and returns one part's arrays. A program takes and returns all parts, laid end to end along the dimension named above; an argument that names none is the same for every part. Nothing has to cross between parts.
Inputs may be any that keep to these rules, and one draw needn't show every extreme that they name: `proc_noise`: symmetric positive definite.
All inputs are finite; a program needn't handle non-finite values. No bound on the sum of `obs_mask` on one device may be relied on, other than what follows from the above.
Results may differ from the reference program's by a relative error of at most 0.00017.
Values sent between devices are 32-bit elements; how exact they have to be, the bound alone decides.
No kernel may reach another device: no remote copies, remote signals or barrier semaphores. Data moves between devices by JAX's collectives and lax.ppermute only.
A program may use at most 128 MiB of HBM per device.

```python
import math
import jax
import jax.numpy as jnp
from jax import lax

S = 128
M = 128
TIME = 16


def draw_transition(key, part):
    rate_key, couple_key = jax.random.split(jax.random.fold_in(key, 11))
    rates = jnp.exp(jax.random.uniform(rate_key, (S,), jnp.float32, math.log(0.3 / TIME), math.log(1.0 / 30.0)))
    couple = jax.random.truncated_normal(couple_key, -3.0, 3.0, (S, S), jnp.float32)
    ident_mat = jnp.eye(S, dtype=jnp.float32)
    return jnp.diag(jnp.exp(-rates)) + couple * (1.0 - ident_mat) * (0.1 / math.sqrt(S))


def draw_proc_noise(key, part):
    level_key, couple_key = jax.random.split(jax.random.fold_in(key, 23))
    levels = jnp.exp(jax.random.uniform(level_key, (S,), jnp.float32, math.log(0.05), math.log(0.5)))
    couple = jax.random.uniform(couple_key, (S, S), jnp.float32, -1.0, 1.0)
    ident_mat = jnp.eye(S, dtype=jnp.float32)
    paired = 0.5 * (couple + couple.T) * (1.0 - ident_mat) * (0.9 * 0.05 / S)
    return jnp.diag(levels) + paired


def place_ends(drawn, key, low, largest):
    longest = drawn.shape.index(max(drawn.shape))
    spots = []
    for shift in (0, 1):
        where = [jax.random.randint(jax.random.fold_in(key, axis), (), 0, length) for axis, length in enumerate(drawn.shape)]
        where[longest] = (where[longest] + shift) % drawn.shape[longest]
        spots.append(tuple(where))
    return drawn.at[spots[0]].set(low).at[spots[1]].set(largest)


def shard_levels(own_key, dims, pieces, low, high):
    def one(position, blocks):
        draws = jax.random.uniform(jax.random.fold_in(jax.random.fold_in(own_key, 6), position), (blocks,), jnp.float32, low / len(pieces), high / len(pieces))
        return jnp.repeat(jnp.exp(draws), dims[position] // blocks).reshape((-1,) + (1,) * (len(dims) - position - 1))

    factor_of = one(*pieces[0])
    for cut in pieces[1:]:
        factor_of = factor_of * one(*cut)
    return factor_of


def gaussian(key, extent, deviation, bound, pieces=(), held_as=jnp.bfloat16):
    result = jax.random.normal(key, extent, jnp.float32) * deviation
    if len(pieces) > 0:
        result = shard_levels(key, extent, pieces, -0.22, 0.18) * result
    return jnp.clip(result, min=-bound, max=bound).astype(held_as)


def setup_inputs(seed: int = 0, part: int = 0) -> dict:
    splits = jax.random.split(jax.random.key(seed), 9)
    part_keys = jax.random.split(jax.random.fold_in(splits[8], part), 9)
    return {
        "observations": gaussian(part_keys[0], (TIME, M), 1.0, 6.0, ((0, 8),), jnp.float32),
        "obs_mask": place_ends((jax.random.randint(part_keys[1], (TIME, M), 0, 4) < 3).astype(jnp.int32), jax.random.fold_in(part_keys[1], 1), 0, 1),
        "sensor_map": place_ends(jax.random.randint(part_keys[2], (M,), 0, S), jax.random.fold_in(part_keys[2], 1), 0, S - 1).astype(jnp.int32),
        "transition": draw_transition(jax.random.fold_in(splits[8], 71), part),
        "proc_noise": draw_proc_noise(jax.random.fold_in(splits[8], 71), part),
        "obs_var": jnp.clip(jnp.exp(jax.random.uniform(splits[5], (M,), jnp.float32, math.log(0.1), math.log(1.0))), 0.1, 1.0),
        "prior_mean": gaussian(part_keys[6], (S,), 1.0, 6.0, (), jnp.float32),
        "prior_var": jnp.clip(jnp.exp(jax.random.uniform(part_keys[7], (S,), jnp.float32, math.log(0.5), math.log(4.0))), 0.5, 4.0),
    }


def highest(left, right):
    return jnp.dot(left, right, precision=lax.Precision.HIGHEST)

def filter_step(carried, inputs, transition, proc_noise, sensor_map, obs_var):
    prev_mean, prev_cov = carried
    observed, mask_row = inputs
    weights = mask_row.astype(jnp.float32)
    pred_mean = highest(transition, prev_mean)
    pred_cov = highest(highest(transition, prev_cov), transition.T) + proc_noise
    picked = pred_cov[sensor_map] * weights[:, None]
    innov_cov = picked[:, sensor_map] * weights[None, :] + jnp.diag(obs_var)
    factor = jnp.linalg.cholesky(innov_cov)
    solved = jax.scipy.linalg.cho_solve((factor, True), picked)
    innovation = weights * (observed - pred_mean[sensor_map])
    new_mean = pred_mean + highest(solved.T, innovation)
    new_cov = pred_cov - highest(picked.T, solved)
    new_cov = 0.5 * (new_cov + new_cov.T)
    return ((new_mean, new_cov), (new_mean, new_cov))

def reference(observations, obs_mask, sensor_map, transition, proc_noise, obs_var, prior_mean, prior_var):
    start_state = (prior_mean, jnp.diag(prior_var))

    def advance(carried, inputs):
        return filter_step(carried, inputs, transition, proc_noise, sensor_map, obs_var)
    last_state, outputs = lax.scan(advance, start_state, (observations, obs_mask))
    return (outputs[0], outputs[1])
```

```python
import jax
import jax.numpy as jnp
from jax import lax
from jax.experimental import pallas as pl
from jax.experimental.pallas import tpu as pltpu
from jax.sharding import PartitionSpec as P

SERIES_BOUND = 1e-3
TIME_AXES = ("outer", "inner")


def split(value):
    high = value.astype(jnp.bfloat16)
    return high, (value - high.astype(jnp.float32)).astype(jnp.bfloat16)


def dot3(left, right):
    left_high, left_low = split(left)
    right_high, right_low = split(right)

    def product(a, b):
        return jnp.dot(a, b, preferred_element_type=jnp.float32)

    return product(left_high, right_high) + (
        product(left_high, right_low) + product(left_low, right_high)
    )


def dot_full(left, right):
    return lax.dot_general(
        left, right, (((1,), (0,)), ((), ())),
        precision=lax.Precision.HIGHEST, preferred_element_type=jnp.float32,
    )


def dot_full_nt(left, right):
    return lax.dot_general(
        left, right, (((1,), (1,)), ((), ())),
        precision=lax.Precision.HIGHEST, preferred_element_type=jnp.float32,
    )


def gather_steps(rows, parts):
    gathered = rows[None]
    reach = 1
    while reach < parts:
        pairs = [(i, i ^ reach) for i in range(parts)]
        gathered = jnp.concatenate([gathered, lax.ppermute(gathered, TIME_AXES, pairs)], 0)
        reach *= 2
    return gathered


def kernel(
    own_ref, steps_ref, map_ref, trans_ref, noise_ref, var_ref, mean_ref, prior_ref,
    mean_out, cov_out, prec_ref, info_ref, state_ref, check_ref, trans_t_ref,
):
    parts, rows_each, width = steps_ref.shape
    per_part = rows_each // 2
    size = trans_ref.shape[0]
    own = own_ref[0]
    first = own * per_part
    row_ids = lax.broadcasted_iota(jnp.int32, (size, size), 0)
    col_ids = lax.broadcasted_iota(jnp.int32, (size, size), 1)
    on_diag = row_ids == col_ids

    inv_var = 1.0 / var_ref[...]

    def place(source, carried):
        block = steps_ref[source ^ own]
        weight = block[per_part:] * inv_var
        prec_ref[pl.ds(source * per_part, per_part), :] = weight
        info_ref[pl.ds(source * per_part, per_part), :] = weight * block[:per_part]
        return carried

    lax.fori_loop(0, parts, place, 0, unroll=parts <= 8)
    chosen = (row_ids == map_ref[...]).astype(jnp.float32)
    prec_ref[...] = dot_full_nt(prec_ref[...], chosen)
    info_ref[...] = dot_full_nt(info_ref[...], chosen)

    trans = trans_ref[...]
    noise = noise_ref[...]
    trans_t = trans.T
    trans_t_ref[...] = trans_t
    pad = jnp.zeros((7, size), jnp.float32)
    check_ref[...] = jnp.zeros_like(check_ref)

    def start():
        cov = dot3(trans * prior_ref[...], trans_t_ref[...]) + noise
        mean = dot3(jnp.broadcast_to(mean_ref[...], (8, size)), trans_t_ref[...])
        return cov, mean

    def factors(cov, mean, step):
        prec = prec_ref[pl.ds(step, 1), :]
        info = info_ref[pl.ds(step, 1), :]
        own_var = jnp.sum(jnp.where(on_diag, cov, 0.0), axis=0, keepdims=True)
        shrink = 1.0 / (1.0 + own_var * prec)
        series = jnp.where(on_diag, 0.0, cov * (prec * shrink))
        push = (info - prec * mean) * shrink
        return shrink, series, push

    def advance(cov, mean, step, outs):
        shrink, series, push = factors(cov, mean, step)
        trans_t = trans_t_ref[...]
        left = [trans_ref[...] * shrink, push]
        if outs:
            left.append(jnp.where(on_diag, jnp.broadcast_to(shrink, (size, size)), 0.0))
        left = jnp.concatenate(left, 0)
        first_pow = dot3(jnp.concatenate([series, left], 0), series)
        pow2, left1 = first_pow[:size], first_pow[size:]
        moved = dot3(jnp.concatenate([cov, mean], 0), trans_t)
        right0, mean0 = moved[:size], moved[size:]
        second = dot3(jnp.concatenate([pow2, series, left1], 0), pow2)
        pow4, pow3, left3 = second[:size], second[size : 2 * size], second[2 * size :]
        check_ref[step] = jnp.sum((pow4 * pow4).reshape(size // 8, 8, size), axis=0)
        left = left - left3
        left = left + dot3(left, 2.0 * pow2 - series - pow3 + pow4)
        even = pow4 - pow2
        if outs:
            right0 = jnp.concatenate([right0, cov], 1)
        right = right0 + dot3(even, right0)
        final = dot3(left[: size + 8], right[:, :size])
        cov_next, mean_next = final[:size] + noise_ref[...], final[size:] + mean0
        if not outs:
            return cov_next, mean_next
        filt = dot3(left[size:], right[:, size:])
        return cov_next, mean_next, filt[8:], filt[:8] + mean

    cov, mean = start()

    def body(step, carried):
        return advance(*carried, step, False)

    cov, mean = lax.fori_loop(0, first, body, (cov, mean))
    for j in range(per_part):
        cov, mean, filt_cov, filt_mean = advance(cov, mean, first + j, True)
        cov_out[j] = 0.5 * (filt_cov + filt_cov.T)
        mean_out[pl.ds(j, 1), :] = filt_mean[:1]

    sizes = jnp.sum(jnp.sum(check_ref[...], axis=1), axis=1, keepdims=True)
    failed = jnp.sum(jnp.where(sizes <= SERIES_BOUND, 0.0, 1.0))

    @pl.when(failed > 0.0)
    def _():
        lane = lax.broadcasted_iota(jnp.int32, (1, size), 1)

        def absorb(step, mean):
            prec = prec_ref[pl.ds(step, 1), :]
            info = info_ref[pl.ds(step, 1), :]

            def one(s, mean):
                here = lane == s

                def at(row):
                    return jnp.sum(jnp.where(here, row, 0.0), axis=1, keepdims=True)

                cov = state_ref[...]
                row = state_ref[pl.ds(s, 1), :]
                col = jnp.sum(jnp.where(here, cov, 0.0), axis=1, keepdims=True)
                scale = 1.0 / (1.0 + at(prec) * at(row))
                state_ref[...] = cov - col * (row * (at(prec) * scale))
                return mean + row * ((at(info) - at(prec) * at(mean)) * scale)

            mean = lax.fori_loop(0, size, one, mean)
            cov = state_ref[...]
            state_ref[...] = 0.5 * (cov + cov.T)
            return mean

        def predict(mean):
            cov = dot_full(dot_full(trans_ref[...], state_ref[...]), trans_t_ref[...])
            state_ref[...] = cov + noise_ref[...]
            return dot_full(jnp.broadcast_to(mean, (8, size)), trans_t_ref[...])[:1]

        state_ref[...] = dot_full(trans_ref[...] * prior_ref[...], trans_t_ref[...]) + noise_ref[...]
        mean = dot_full(jnp.broadcast_to(mean_ref[...], (8, size)), trans_t_ref[...])[:1]
        mean = lax.fori_loop(0, first, lambda t, m: predict(absorb(t, m)), mean)
        for j in range(per_part):
            mean = absorb(first + j, mean)
            cov_out[j] = state_ref[...]
            mean_out[pl.ds(j, 1), :] = mean
            if j + 1 < per_part:
                mean = predict(mean)


def local(
    observations, obs_mask, sensor_map, transition, proc_noise, obs_var, prior_mean, prior_var
):
    steps_here, sensors = observations.shape
    size = transition.shape[0]
    parts = lax.axis_size("outer") * lax.axis_size("inner")
    position = lax.axis_index("outer") * lax.axis_size("inner") + lax.axis_index("inner")
    rows = jnp.concatenate([observations, obs_mask.astype(jnp.float32)], 0)
    gathered = gather_steps(rows, parts)
    steps = parts * steps_here
    vmem = pl.BlockSpec(memory_space=pltpu.VMEM)
    return pl.pallas_call(
        kernel,
        out_shape=(
            jax.ShapeDtypeStruct((steps_here, size), jnp.float32),
            jax.ShapeDtypeStruct((steps_here, size, size), jnp.float32),
        ),
        in_specs=[pl.BlockSpec(memory_space=pltpu.SMEM)] + [vmem] * 7,
        out_specs=(vmem, vmem),
        scratch_shapes=[
            pltpu.VMEM((steps, sensors), jnp.float32),
            pltpu.VMEM((steps, sensors), jnp.float32),
            pltpu.VMEM((size, size), jnp.float32),
            pltpu.VMEM((steps, 8, size), jnp.float32),
            pltpu.VMEM((size, size), jnp.float32),
        ],
        name="filter_window",
    )(
        position.astype(jnp.int32)[None], gathered, sensor_map[None], transition, proc_noise,
        obs_var[None], prior_mean[None], prior_var[None],
    )


def solution(mesh):
    return jax.shard_map(
        local,
        mesh=mesh,
        in_specs=(
            P(("region", "outer", "inner"), None),
            P(("region", "outer", "inner"), None),
            P("region"),
            P(),
            P(),
            P(),
            P("region"),
            P("region"),
        ),
        out_specs=(
            P(("region", "outer", "inner"), None),
            P(("region", "outer", "inner"), None, None),
        ),
        check_vma=False,
    )
```

```python
import math

import jax
import jax.numpy as jnp
from jax import lax
from jax.experimental import pallas as pl
from jax.experimental.pallas import tpu as pltpu
from jax.sharding import PartitionSpec as P

RADIUS = 0.6
SERIES_BOUND = RADIUS**8
TIME_AXES = ("outer", "inner")


def series_factors():
    squeeze = 1.0 - RADIUS**2

    def quartic(k):
        cosine = math.cos(k * math.pi / 6)
        const = cosine**2 + squeeze * math.sin(k * math.pi / 6) ** 2
        return 2.0 * const - 4.0 * cosine**2, const**2

    return squeeze, quartic(2), quartic(1)


def split(value):
    high = value.astype(jnp.bfloat16)
    return high, (value - high.astype(jnp.float32)).astype(jnp.bfloat16)


def mul(left, right):
    size = right[0].shape[1]
    columns = jnp.concatenate(right, 1)
    result = jnp.dot(
        jnp.concatenate(left, 1),
        jnp.concatenate([columns, columns], 0),
        preferred_element_type=jnp.float32,
    )
    return result[:, :size] + result[:, size:]


def dot3(left, right):
    return mul(split(left), split(right))


def dot_full(left, right):
    return lax.dot_general(
        left, right, (((1,), (0,)), ((), ())),
        precision=lax.Precision.HIGHEST, preferred_element_type=jnp.float32,
    )


def dot_full_nt(left, right):
    return lax.dot_general(
        left, right, (((1,), (1,)), ((), ())),
        precision=lax.Precision.HIGHEST, preferred_element_type=jnp.float32,
    )


def gather_steps(rows, parts):
    gathered = rows[None]
    reach = 1
    while reach < parts:
        pairs = [(i, i ^ reach) for i in range(parts)]
        gathered = jnp.concatenate([gathered, lax.ppermute(gathered, TIME_AXES, pairs)], 0)
        reach *= 2
    return gathered


def kernel(
    own_ref, steps_ref, map_ref, trans_ref, noise_ref, var_ref, mean_ref, prior_ref,
    mean_out, cov_out, prec_ref, info_ref, state_ref, check_ref, trans_t_ref,
):
    parts, rows_each, width = steps_ref.shape
    per_part = rows_each // 2
    size = trans_ref.shape[0]
    own = own_ref[0]
    first = own * per_part
    row_ids = lax.broadcasted_iota(jnp.int32, (size, size), 0)
    col_ids = lax.broadcasted_iota(jnp.int32, (size, size), 1)
    on_diag = row_ids == col_ids

    inv_var = 1.0 / var_ref[...]

    def place(source, carried):
        block = steps_ref[source ^ own]
        weight = block[per_part:] * inv_var
        prec_ref[pl.ds(source * per_part, per_part), :] = weight
        info_ref[pl.ds(source * per_part, per_part), :] = weight * block[:per_part]
        return carried

    lax.fori_loop(0, parts, place, 0, unroll=parts <= 8)
    chosen = (row_ids == map_ref[...]).astype(jnp.float32)
    prec_ref[...] = dot_full_nt(prec_ref[...], chosen)
    info_ref[...] = dot_full_nt(info_ref[...], chosen)

    trans = trans_ref[...]
    noise = noise_ref[...]
    trans_t = trans.T
    trans_t_ref[...] = trans_t
    pad = jnp.zeros((7, size), jnp.float32)
    check_ref[...] = jnp.zeros_like(check_ref)

    def start():
        cov = dot3(trans * prior_ref[...], trans_t_ref[...]) + noise
        mean = dot3(jnp.broadcast_to(mean_ref[...], (8, size)), trans_t_ref[...])
        return cov, mean

    def factors(cov, mean, step):
        prec = prec_ref[pl.ds(step, 1), :]
        info = info_ref[pl.ds(step, 1), :]
        own_var = jnp.sum(jnp.where(on_diag, cov, 0.0), axis=0, keepdims=True)
        shrink = 1.0 / (1.0 + own_var * prec)
        series = jnp.where(on_diag, 0.0, cov * (prec * shrink))
        push = (info - prec * mean) * shrink
        return shrink, series, push

    square, wide, narrow = series_factors()

    def advance(cov, mean, step, move, outs):
        shrink, series, push = factors(cov, mean, step)
        series = split(series)
        pow2 = mul(series, series)
        lefts = []
        rights = []
        if move:
            lefts.append(trans_ref[...] * shrink)
            moved = mul(split(jnp.concatenate([cov, mean], 0)), split(trans_t_ref[...]))
            rights.append(moved[:size])
        if outs:
            lefts.append(jnp.where(on_diag, jnp.broadcast_to(shrink, (size, size)), 0.0))
            rights.append(cov)
        lefts[-1] = jnp.concatenate([lefts[-1], push], 0)
        pow2_split = split(pow2)
        pow4 = jnp.dot(pow2_split[0], pow2_split[0], preferred_element_type=jnp.float32)
        check_ref[step] = jnp.sum((pow4 * pow4).reshape(size // 8, 8, size), axis=0)
        even_left = split(pow4 * (1.0 / wide[1]) + pow2 * (wide[0] / wide[1]))
        even_right = split(pow4 * (1.0 / narrow[1]) + pow2 * (narrow[0] / narrow[1]))
        pow2_scaled = split(pow2 * (1.0 / square))
        done = []
        for left in lefts:
            left = left - mul(split(left), series)
            left = left + mul(split(left), pow2_scaled)
            done.append(split(left + mul(split(left), even_left)))
        rights = [split(right + mul(even_right, split(right))) for right in rights]
        result = []
        if move:
            final = mul(done[0], rights[0])
            mean_next = final[size:] if not outs else mul(tuple(x[size:] for x in done[1]), rights[0])
            result += [final[:size] + noise_ref[...], mean_next + moved[size:]]
        if outs:
            final = mul(done[-1], rights[-1])
            result += [final[:size], final[size:] + mean]
        return result

    cov, mean = start()

    def body(step, carried):
        return tuple(advance(*carried, step, True, False))

    cov, mean = lax.fori_loop(0, first, body, (cov, mean))
    for j in range(per_part):
        moves = j + 1 < per_part
        result = advance(cov, mean, first + j, moves, True)
        if moves:
            cov, mean = result[:2]
        filt_cov, filt_mean = result[-2:]
        cov_out[j] = 0.5 * (filt_cov + filt_cov.T)
        mean_out[pl.ds(j, 1), :] = filt_mean[:1]

    sizes = jnp.sum(jnp.sum(check_ref[...], axis=1), axis=1, keepdims=True)
    failed = jnp.sum(jnp.where(sizes <= SERIES_BOUND, 0.0, 1.0))

    @pl.when(failed > 0.0)
    def _():
        lane = lax.broadcasted_iota(jnp.int32, (1, size), 1)

        def absorb(step, mean):
            prec = prec_ref[pl.ds(step, 1), :]
            info = info_ref[pl.ds(step, 1), :]

            def one(s, mean):
                here = lane == s

                def at(row):
                    return jnp.sum(jnp.where(here, row, 0.0), axis=1, keepdims=True)

                cov = state_ref[...]
                row = state_ref[pl.ds(s, 1), :]
                col = jnp.sum(jnp.where(here, cov, 0.0), axis=1, keepdims=True)
                scale = 1.0 / (1.0 + at(prec) * at(row))
                state_ref[...] = cov - col * (row * (at(prec) * scale))
                return mean + row * ((at(info) - at(prec) * at(mean)) * scale)

            mean = lax.fori_loop(0, size, one, mean)
            cov = state_ref[...]
            state_ref[...] = 0.5 * (cov + cov.T)
            return mean

        def predict(mean):
            cov = dot_full(dot_full(trans_ref[...], state_ref[...]), trans_t_ref[...])
            state_ref[...] = cov + noise_ref[...]
            return dot_full(jnp.broadcast_to(mean, (8, size)), trans_t_ref[...])[:1]

        state_ref[...] = dot_full(trans_ref[...] * prior_ref[...], trans_t_ref[...]) + noise_ref[...]
        mean = dot_full(jnp.broadcast_to(mean_ref[...], (8, size)), trans_t_ref[...])[:1]
        mean = lax.fori_loop(0, first, lambda t, m: predict(absorb(t, m)), mean)
        for j in range(per_part):
            mean = absorb(first + j, mean)
            cov_out[j] = state_ref[...]
            mean_out[pl.ds(j, 1), :] = mean
            if j + 1 < per_part:
                mean = predict(mean)


def local(
    observations, obs_mask, sensor_map, transition, proc_noise, obs_var, prior_mean, prior_var
):
    steps_here, sensors = observations.shape
    size = transition.shape[0]
    parts = lax.axis_size("outer") * lax.axis_size("inner")
    position = lax.axis_index("outer") * lax.axis_size("inner") + lax.axis_index("inner")
    rows = jnp.concatenate([observations, obs_mask.astype(jnp.float32)], 0)
    gathered = gather_steps(rows, parts)
    steps = parts * steps_here
    vmem = pl.BlockSpec(memory_space=pltpu.VMEM)
    return pl.pallas_call(
        kernel,
        out_shape=(
            jax.ShapeDtypeStruct((steps_here, size), jnp.float32),
            jax.ShapeDtypeStruct((steps_here, size, size), jnp.float32),
        ),
        in_specs=[pl.BlockSpec(memory_space=pltpu.SMEM)] + [vmem] * 7,
        out_specs=(vmem, vmem),
        scratch_shapes=[
            pltpu.VMEM((steps, sensors), jnp.float32),
            pltpu.VMEM((steps, sensors), jnp.float32),
            pltpu.VMEM((size, size), jnp.float32),
            pltpu.VMEM((steps, 8, size), jnp.float32),
            pltpu.VMEM((size, size), jnp.float32),
        ],
        name="filter_window",
    )(
        position.astype(jnp.int32)[None], gathered, sensor_map[None], transition, proc_noise,
        obs_var[None], prior_mean[None], prior_var[None],
    )


def solution(mesh):
    return jax.shard_map(
        local,
        mesh=mesh,
        in_specs=(
            P(("region", "outer", "inner"), None),
            P(("region", "outer", "inner"), None),
            P("region"),
            P(),
            P(),
            P(),
            P("region"),
            P("region"),
        ),
        out_specs=(
            P(("region", "outer", "inner"), None),
            P(("region", "outer", "inner"), None, None),
        ),
        check_vma=False,
    )
```

```python
import math

import jax
import jax.numpy as jnp
from jax import lax
from jax.experimental import pallas as pl
from jax.experimental.pallas import tpu as pltpu
from jax.sharding import PartitionSpec as P

RADIUS = 0.6
SERIES_BOUND = RADIUS**8
TIME_AXES = ("outer", "inner")


def series_factors():
    squeeze = 1.0 - RADIUS**2

    def quartic(k):
        cosine = math.cos(k * math.pi / 6)
        const = cosine**2 + squeeze * math.sin(k * math.pi / 6) ** 2
        return 2.0 * const - 4.0 * cosine**2, const**2

    return squeeze, quartic(2), quartic(1)


def split(value):
    high = value.astype(jnp.bfloat16)
    return high, (value - high.astype(jnp.float32)).astype(jnp.bfloat16)


def mul(left, right):
    size = right[0].shape[1]
    columns = jnp.concatenate(right, 1)
    result = jnp.dot(
        jnp.concatenate(left, 1),
        jnp.concatenate([columns, columns], 0),
        preferred_element_type=jnp.float32,
    )
    return result[:, :size] + result[:, size:]


def dot3(left, right):
    return mul(split(left), split(right))


def dot_full(left, right):
    return lax.dot_general(
        left, right, (((1,), (0,)), ((), ())),
        precision=lax.Precision.HIGHEST, preferred_element_type=jnp.float32,
    )


def gather_steps(rows, parts):
    gathered = rows[None]
    reach = 1
    while reach < parts:
        pairs = [(i, i ^ reach) for i in range(parts)]
        gathered = jnp.concatenate([gathered, lax.ppermute(gathered, TIME_AXES, pairs)], 0)
        reach *= 2
    return gathered


def prepare(
    map_ref, var_ref, trans_ref, noise_ref, mean_ref, prior_ref,
    start_ref, turned_ref, chosen_ref, inv_var_ref,
):
    size = trans_ref.shape[0]
    sensors = map_ref.shape[1]
    trans = trans_ref[...]
    turned = trans.T
    turned_ref[...] = turned
    rows = jnp.concatenate(
        [trans * prior_ref[...], jnp.broadcast_to(mean_ref[...], (8, size))], 0
    )
    rows = dot3(rows, turned)
    start_ref[:size] = rows[:size] + noise_ref[...]
    start_ref[size:] = rows[size:]
    components = lax.broadcasted_iota(jnp.int32, (size, sensors), 0)
    chosen = (components == map_ref[...]).astype(jnp.float32)
    chosen_ref[...] = chosen.T
    inv_var_ref[...] = 1.0 / var_ref[...]


def kernel(
    own_ref, steps_ref, start_ref, turned_ref, chosen_ref, inv_var_ref, trans_ref, noise_ref,
    mean_ref, prior_ref, mean_out, cov_out, prec_ref, info_ref, state_ref, check_ref, high_ref,
    low_ref,
):
    parts, rows_each, width = steps_ref.shape
    per_part = rows_each // 2
    steps = parts * per_part
    size = trans_ref.shape[0]
    own = own_ref[0]
    first = own * per_part
    row_ids = lax.broadcasted_iota(jnp.int32, (size, size), 0)
    col_ids = lax.broadcasted_iota(jnp.int32, (size, size), 1)
    on_diag = row_ids == col_ids

    inv_var = inv_var_ref[...]

    def place(source, carried):
        block = steps_ref[source ^ own]
        weight = block[per_part:] * inv_var
        prec_ref[pl.ds(source * per_part, per_part), :] = weight
        info_ref[pl.ds(source * per_part, per_part), :] = weight * block[:per_part]
        return carried

    lax.fori_loop(0, parts, place, 0, unroll=parts <= 8)
    chosen = chosen_ref[...].astype(jnp.bfloat16)
    left = jnp.concatenate([prec_ref[...], info_ref[...]], 0)
    summed = jnp.zeros(left.shape, jnp.float32)
    for _ in range(3):
        part = left.astype(jnp.bfloat16)
        left = left - part.astype(jnp.float32)
        summed = summed + jnp.dot(part, chosen, preferred_element_type=jnp.float32)
    prec_ref[...] = summed[:steps]
    info_ref[...] = summed[steps:]
    high_ref[...], low_ref[...] = split(turned_ref[...])
    check_ref[...] = jnp.zeros_like(check_ref)

    def factors(cov, mean, step):
        prec = prec_ref[pl.ds(step, 1), :]
        info = info_ref[pl.ds(step, 1), :]
        own_var = jnp.sum(jnp.where(on_diag, cov, 0.0), axis=0, keepdims=True)
        shrink = 1.0 / (1.0 + own_var * prec)
        series = jnp.where(on_diag, 0.0, cov * (prec * shrink))
        push = (info - prec * mean) * shrink
        return shrink, series, push

    square, wide, narrow = series_factors()
    whole = 1.0 / (square * wide[1] * narrow[1])

    def advance(cov, mean, step, move, outs):
        shrink, series, push = factors(cov, mean, step)
        series = split(series)
        pow2 = mul(series, series)
        lefts = []
        rights = []
        if move:
            lefts.append(trans_ref[...] * (shrink * whole))
            moved = mul(split(jnp.concatenate([cov, mean], 0)), (high_ref[...], low_ref[...]))
            rights.append(moved[:size])
        if outs:
            lefts.append(jnp.where(on_diag, jnp.broadcast_to(shrink * whole, (size, size)), 0.0))
            rights.append(cov)
        lefts[-1] = jnp.concatenate([lefts[-1], push * whole], 0)
        pow2_split = split(pow2)
        pow4 = jnp.dot(pow2_split[0], pow2_split[0], preferred_element_type=jnp.float32)
        check_ref[step] = jnp.sum((pow4 * pow4).reshape(size // 8, 8, size), axis=0)
        even_left = split(pow4 + pow2 * wide[0])
        even_right = split(pow4 + pow2 * narrow[0])
        done = []
        for left in lefts:
            left = left - mul(split(left), series)
            left = left * square + mul(split(left), pow2_split)
            done.append(split(left * wide[1] + mul(split(left), even_left)))
        rights = [split(right * narrow[1] + mul(even_right, split(right))) for right in rights]
        result = []
        if move:
            final = mul(done[0], rights[0])
            mean_next = final[size:] if not outs else mul(tuple(x[size:] for x in done[1]), rights[0])
            result += [final[:size] + noise_ref[...], mean_next + moved[size:]]
        if outs:
            final = mul(done[-1], rights[-1])
            result += [final[:size], final[size:] + mean]
        return result

    cov, mean = start_ref[:size], start_ref[size:]

    def body(step, carried):
        return tuple(advance(*carried, step, True, False))

    cov, mean = lax.fori_loop(0, first, body, (cov, mean))
    for j in range(per_part):
        moves = j + 1 < per_part
        result = advance(cov, mean, first + j, moves, True)
        if moves:
            cov, mean = result[:2]
        filt_cov, filt_mean = result[-2:]
        cov_out[j] = 0.5 * (filt_cov + filt_cov.T)
        mean_out[pl.ds(j, 1), :] = filt_mean[:1]

    sizes = jnp.sum(jnp.sum(check_ref[...], axis=1), axis=1, keepdims=True)
    failed = jnp.sum(jnp.where(sizes <= SERIES_BOUND, 0.0, 1.0))

    @pl.when(failed > 0.0)
    def _():
        lane = lax.broadcasted_iota(jnp.int32, (1, size), 1)

        def absorb(step, mean):
            prec = prec_ref[pl.ds(step, 1), :]
            info = info_ref[pl.ds(step, 1), :]

            def one(s, mean):
                here = lane == s

                def at(row):
                    return jnp.sum(jnp.where(here, row, 0.0), axis=1, keepdims=True)

                cov = state_ref[...]
                row = state_ref[pl.ds(s, 1), :]
                col = jnp.sum(jnp.where(here, cov, 0.0), axis=1, keepdims=True)
                scale = 1.0 / (1.0 + at(prec) * at(row))
                state_ref[...] = cov - col * (row * (at(prec) * scale))
                return mean + row * ((at(info) - at(prec) * at(mean)) * scale)

            mean = lax.fori_loop(0, size, one, mean)
            cov = state_ref[...]
            state_ref[...] = 0.5 * (cov + cov.T)
            return mean

        def predict(mean):
            cov = dot_full(dot_full(trans_ref[...], state_ref[...]), turned_ref[...])
            state_ref[...] = cov + noise_ref[...]
            return dot_full(jnp.broadcast_to(mean, (8, size)), turned_ref[...])[:1]

        state_ref[...] = dot_full(trans_ref[...] * prior_ref[...], turned_ref[...]) + noise_ref[...]
        mean = dot_full(jnp.broadcast_to(mean_ref[...], (8, size)), turned_ref[...])[:1]
        mean = lax.fori_loop(0, first, lambda t, m: predict(absorb(t, m)), mean)
        for j in range(per_part):
            mean = absorb(first + j, mean)
            cov_out[j] = state_ref[...]
            mean_out[pl.ds(j, 1), :] = mean
            if j + 1 < per_part:
                mean = predict(mean)


def local(
    observations, obs_mask, sensor_map, transition, proc_noise, obs_var, prior_mean, prior_var
):
    steps_here, sensors = observations.shape
    size = transition.shape[0]
    parts = lax.axis_size("outer") * lax.axis_size("inner")
    position = lax.axis_index("outer") * lax.axis_size("inner") + lax.axis_index("inner")
    rows = jnp.concatenate([observations, obs_mask.astype(jnp.float32)], 0)
    gathered = gather_steps(rows, parts)
    steps = parts * steps_here
    vmem = pl.BlockSpec(memory_space=pltpu.VMEM)

    def near(*arrays):
        return [pltpu.with_memory_space_constraint(a, pltpu.VMEM) for a in arrays]

    transition, proc_noise, prior_mean, prior_var = near(
        transition, proc_noise, prior_mean[None], prior_var[None]
    )
    prepared = pl.pallas_call(
        prepare,
        out_shape=(
            pltpu.VMEM((size + 8, size), jnp.float32),
            pltpu.VMEM((size, size), jnp.float32),
            pltpu.VMEM((sensors, size), jnp.float32),
            pltpu.VMEM((1, sensors), jnp.float32),
        ),
        in_specs=[vmem] * 6,
        out_specs=(vmem,) * 4,
        name="prepare_window",
    )(*near(sensor_map[None], obs_var[None]), transition, proc_noise, prior_mean, prior_var)
    return pl.pallas_call(
        kernel,
        out_shape=(
            jax.ShapeDtypeStruct((steps_here, size), jnp.float32),
            jax.ShapeDtypeStruct((steps_here, size, size), jnp.float32),
        ),
        in_specs=[pl.BlockSpec(memory_space=pltpu.SMEM)] + [vmem] * 9,
        out_specs=(vmem, vmem),
        scratch_shapes=[
            pltpu.VMEM((steps, sensors), jnp.float32),
            pltpu.VMEM((steps, sensors), jnp.float32),
            pltpu.VMEM((size, size), jnp.float32),
            pltpu.VMEM((steps, 8, size), jnp.float32),
            pltpu.VMEM((size, size), jnp.bfloat16),
            pltpu.VMEM((size, size), jnp.bfloat16),
        ],
        name="filter_window",
    )(
        position.astype(jnp.int32)[None], *near(gathered, *prepared), transition, proc_noise,
        prior_mean, prior_var,
    )


def solution(mesh):
    return jax.shard_map(
        local,
        mesh=mesh,
        in_specs=(
            P(("region", "outer", "inner"), None),
            P(("region", "outer", "inner"), None),
            P("region"),
            P(),
            P(),
            P(),
            P("region"),
            P("region"),
        ),
        out_specs=(
            P(("region", "outer", "inner"), None),
            P(("region", "outer", "inner"), None, None),
        ),
        check_vma=False,
    )
```

```python
import math

import jax
import jax.numpy as jnp
from jax import lax
from jax.experimental import pallas as pl
from jax.experimental.pallas import tpu as pltpu
from jax.sharding import PartitionSpec as P

RADIUS = 0.6
SERIES_BOUND = RADIUS**8
TIME_AXES = ("outer", "inner")


def series_factors():
    squeeze = 1.0 - RADIUS**2

    def quartic(k):
        cosine = math.cos(k * math.pi / 6)
        const = cosine**2 + squeeze * math.sin(k * math.pi / 6) ** 2
        return 2.0 * const - 4.0 * cosine**2, const**2

    return squeeze, quartic(2), quartic(1)


def split(value):
    high = value.astype(jnp.bfloat16)
    return high, (value - high.astype(jnp.float32)).astype(jnp.bfloat16)


def mul(left, right):
    size = right[0].shape[1]
    columns = jnp.concatenate(right, 1)
    result = jnp.dot(
        jnp.concatenate(left, 1),
        jnp.concatenate([columns, columns], 0),
        preferred_element_type=jnp.float32,
    )
    return result[:, :size] + result[:, size:]


def dot3(left, right):
    return mul(split(left), split(right))


def dot_full(left, right):
    return lax.dot_general(
        left, right, (((1,), (0,)), ((), ())),
        precision=lax.Precision.HIGHEST, preferred_element_type=jnp.float32,
    )


def gather_steps(rows, parts):
    gathered = rows[None]
    reach = 1
    while reach < parts:
        pairs = [(i, i ^ reach) for i in range(parts)]
        gathered = jnp.concatenate([gathered, lax.ppermute(gathered, TIME_AXES, pairs)], 0)
        reach *= 2
    return gathered


def prepare(
    map_ref, var_ref, trans_ref, noise_ref, mean_ref, prior_ref,
    start_ref, turned_ref, chosen_ref, inv_var_ref, trans_out, noise_out, mean_out, prior_out,
):
    size = trans_ref.shape[0]
    sensors = map_ref.shape[1]
    trans = trans_ref[...]
    turned = trans.T
    turned_ref[...] = turned
    rows = jnp.concatenate(
        [trans * prior_ref[...], jnp.broadcast_to(mean_ref[...], (8, size))], 0
    )
    rows = dot3(rows, turned)
    start_ref[:size] = rows[:size] + noise_ref[...]
    start_ref[size:] = rows[size:]
    components = lax.broadcasted_iota(jnp.int32, (size, sensors), 0)
    chosen = (components == map_ref[...]).astype(jnp.float32)
    chosen_ref[...] = chosen.T
    inv_var_ref[...] = 1.0 / var_ref[...]
    trans_out[...] = trans
    noise_out[...] = noise_ref[...]
    mean_out[...] = mean_ref[...]
    prior_out[...] = prior_ref[...]


def kernel(
    own_ref, steps_ref, start_ref, turned_ref, chosen_ref, inv_var_ref, trans_ref, noise_ref,
    mean_ref, prior_ref, mean_out, cov_out, prec_ref, info_ref, state_ref, check_ref, high_ref,
    low_ref,
):
    parts, rows_each, width = steps_ref.shape
    per_part = rows_each // 2
    steps = parts * per_part
    size = trans_ref.shape[0]
    own = own_ref[0]
    first = own * per_part
    row_ids = lax.broadcasted_iota(jnp.int32, (size, size), 0)
    col_ids = lax.broadcasted_iota(jnp.int32, (size, size), 1)
    on_diag = row_ids == col_ids

    inv_var = inv_var_ref[...]

    def place(source, carried):
        block = steps_ref[source ^ own]
        weight = block[per_part:] * inv_var
        prec_ref[pl.ds(source * per_part, per_part), :] = weight
        info_ref[pl.ds(source * per_part, per_part), :] = weight * block[:per_part]
        return carried

    lax.fori_loop(0, parts, place, 0, unroll=parts <= 8)
    chosen = chosen_ref[...].astype(jnp.bfloat16)
    left = jnp.concatenate([prec_ref[...], info_ref[...]], 0)
    summed = jnp.zeros(left.shape, jnp.float32)
    for _ in range(3):
        part = left.astype(jnp.bfloat16)
        left = left - part.astype(jnp.float32)
        summed = summed + jnp.dot(part, chosen, preferred_element_type=jnp.float32)
    prec_ref[...] = summed[:steps]
    info_ref[...] = summed[steps:]
    high_ref[...], low_ref[...] = split(turned_ref[...])
    check_ref[...] = jnp.zeros_like(check_ref)

    def factors(cov, mean, step):
        prec = prec_ref[pl.ds(step, 1), :]
        info = info_ref[pl.ds(step, 1), :]
        own_var = jnp.sum(jnp.where(on_diag, cov, 0.0), axis=0, keepdims=True)
        shrink = 1.0 / (1.0 + own_var * prec)
        series = jnp.where(on_diag, 0.0, cov * (prec * shrink))
        push = (info - prec * mean) * shrink
        return shrink, series, push

    square, wide, narrow = series_factors()
    whole = 1.0 / (square * wide[1] * narrow[1])

    def advance(cov, mean, step, move, outs):
        shrink, series, push = factors(cov, mean, step)
        series = split(series)
        pow2 = mul(series, series)
        lefts = []
        rights = []
        if move:
            lefts.append(trans_ref[...] * (shrink * whole))
            moved = mul(split(jnp.concatenate([cov, mean], 0)), (high_ref[...], low_ref[...]))
            rights.append(moved[:size])
        if outs:
            lefts.append(jnp.where(on_diag, jnp.broadcast_to(shrink * whole, (size, size)), 0.0))
            rights.append(cov)
        lefts[-1] = jnp.concatenate([lefts[-1], push * whole], 0)
        pow2_split = split(pow2)
        pow4 = jnp.dot(pow2_split[0], pow2_split[0], preferred_element_type=jnp.float32)
        check_ref[step] = jnp.sum((pow4 * pow4).reshape(size // 8, 8, size), axis=0)
        even_left = split(pow4 + pow2 * wide[0])
        even_right = split(pow4 + pow2 * narrow[0])
        done = []
        for left in lefts:
            left = left - mul(split(left), series)
            left = left * square + mul(split(left), pow2_split)
            done.append(split(left * wide[1] + mul(split(left), even_left)))
        rights = [split(right * narrow[1] + mul(even_right, split(right))) for right in rights]
        result = []
        if move:
            final = mul(done[0], rights[0])
            mean_next = final[size:] if not outs else mul(tuple(x[size:] for x in done[1]), rights[0])
            result += [final[:size] + noise_ref[...], mean_next + moved[size:]]
        if outs:
            final = mul(done[-1], rights[-1])
            result += [final[:size], final[size:] + mean]
        return result

    cov, mean = start_ref[:size], start_ref[size:]

    def body(step, carried):
        return tuple(advance(*carried, step, True, False))

    cov, mean = lax.fori_loop(0, first, body, (cov, mean))
    for j in range(per_part):
        moves = j + 1 < per_part
        result = advance(cov, mean, first + j, moves, True)
        if moves:
            cov, mean = result[:2]
        filt_cov, filt_mean = result[-2:]
        cov_out[j] = 0.5 * (filt_cov + filt_cov.T)
        mean_out[pl.ds(j, 1), :] = filt_mean[:1]

    sizes = jnp.sum(jnp.sum(check_ref[...], axis=1), axis=1, keepdims=True)
    failed = jnp.sum(jnp.where(sizes <= SERIES_BOUND, 0.0, 1.0))

    @pl.when(failed > 0.0)
    def _():
        lane = lax.broadcasted_iota(jnp.int32, (1, size), 1)

        def absorb(step, mean):
            prec = prec_ref[pl.ds(step, 1), :]
            info = info_ref[pl.ds(step, 1), :]

            def one(s, mean):
                here = lane == s

                def at(row):
                    return jnp.sum(jnp.where(here, row, 0.0), axis=1, keepdims=True)

                cov = state_ref[...]
                row = state_ref[pl.ds(s, 1), :]
                col = jnp.sum(jnp.where(here, cov, 0.0), axis=1, keepdims=True)
                scale = 1.0 / (1.0 + at(prec) * at(row))
                state_ref[...] = cov - col * (row * (at(prec) * scale))
                return mean + row * ((at(info) - at(prec) * at(mean)) * scale)

            mean = lax.fori_loop(0, size, one, mean)
            cov = state_ref[...]
            state_ref[...] = 0.5 * (cov + cov.T)
            return mean

        def predict(mean):
            cov = dot_full(dot_full(trans_ref[...], state_ref[...]), turned_ref[...])
            state_ref[...] = cov + noise_ref[...]
            return dot_full(jnp.broadcast_to(mean, (8, size)), turned_ref[...])[:1]

        state_ref[...] = dot_full(trans_ref[...] * prior_ref[...], turned_ref[...]) + noise_ref[...]
        mean = dot_full(jnp.broadcast_to(mean_ref[...], (8, size)), turned_ref[...])[:1]
        mean = lax.fori_loop(0, first, lambda t, m: predict(absorb(t, m)), mean)
        for j in range(per_part):
            mean = absorb(first + j, mean)
            cov_out[j] = state_ref[...]
            mean_out[pl.ds(j, 1), :] = mean
            if j + 1 < per_part:
                mean = predict(mean)


def local(
    observations, obs_mask, sensor_map, transition, proc_noise, obs_var, prior_mean, prior_var
):
    steps_here, sensors = observations.shape
    size = transition.shape[0]
    parts = lax.axis_size("outer") * lax.axis_size("inner")
    position = lax.axis_index("outer") * lax.axis_size("inner") + lax.axis_index("inner")
    rows = jnp.concatenate([observations, obs_mask.astype(jnp.float32)], 0)
    gathered = gather_steps(rows, parts)
    steps = parts * steps_here
    vmem = pl.BlockSpec(memory_space=pltpu.VMEM)

    def near(*arrays):
        return [pltpu.with_memory_space_constraint(a, pltpu.VMEM) for a in arrays]

    prepared = pl.pallas_call(
        prepare,
        out_shape=(
            pltpu.VMEM((size + 8, size), jnp.float32),
            pltpu.VMEM((size, size), jnp.float32),
            pltpu.VMEM((sensors, size), jnp.float32),
            pltpu.VMEM((1, sensors), jnp.float32),
            pltpu.VMEM((size, size), jnp.float32),
            pltpu.VMEM((size, size), jnp.float32),
            pltpu.VMEM((1, size), jnp.float32),
            pltpu.VMEM((1, size), jnp.float32),
        ),
        in_specs=[vmem] * 6,
        out_specs=(vmem,) * 8,
        name="prepare_window",
    )(sensor_map[None], obs_var[None], transition, proc_noise, prior_mean[None], prior_var[None])
    return pl.pallas_call(
        kernel,
        out_shape=(
            jax.ShapeDtypeStruct((steps_here, size), jnp.float32),
            jax.ShapeDtypeStruct((steps_here, size, size), jnp.float32),
        ),
        in_specs=[pl.BlockSpec(memory_space=pltpu.SMEM)] + [vmem] * 9,
        out_specs=(vmem, vmem),
        scratch_shapes=[
            pltpu.VMEM((steps, sensors), jnp.float32),
            pltpu.VMEM((steps, sensors), jnp.float32),
            pltpu.VMEM((size, size), jnp.float32),
            pltpu.VMEM((steps, 8, size), jnp.float32),
            pltpu.VMEM((size, size), jnp.bfloat16),
            pltpu.VMEM((size, size), jnp.bfloat16),
        ],
        name="filter_window",
    )(
        position.astype(jnp.int32)[None], *near(gathered, *prepared)
    )


def solution(mesh):
    return jax.shard_map(
        local,
        mesh=mesh,
        in_specs=(
            P(("region", "outer", "inner"), None),
            P(("region", "outer", "inner"), None),
            P("region"),
            P(),
            P(),
            P(),
            P("region"),
            P("region"),
        ),
        out_specs=(
            P(("region", "outer", "inner"), None),
            P(("region", "outer", "inner"), None, None),
        ),
        check_vma=False,
    )
```

```python
import functools
import math

import jax
import jax.numpy as jnp
from jax import lax
from jax.experimental import pallas as pl
from jax.experimental.pallas import tpu as pltpu
from jax.sharding import PartitionSpec as P

RADIUS = 0.6
SERIES_BOUND = RADIUS**8
TIME_AXES = ("outer", "inner")


def series_factors():
    squeeze = 1.0 - RADIUS**2

    def quartic(k):
        cosine = math.cos(k * math.pi / 6)
        const = cosine**2 + squeeze * math.sin(k * math.pi / 6) ** 2
        return 2.0 * const - 4.0 * cosine**2, const**2

    return squeeze, quartic(2), quartic(1)


def split(value):
    high = value.astype(jnp.bfloat16)
    return high, (value - high.astype(jnp.float32)).astype(jnp.bfloat16)


def mul(left, right):
    size = right[0].shape[1]
    columns = jnp.concatenate(right, 1)
    result = jnp.dot(
        jnp.concatenate(left, 1),
        jnp.concatenate([columns, columns], 0),
        preferred_element_type=jnp.float32,
    )
    return result[:, :size] + result[:, size:]


def dot3(left, right):
    return mul(split(left), split(right))


def dot_full(left, right):
    return lax.dot_general(
        left, right, (((1,), (0,)), ((), ())),
        precision=lax.Precision.HIGHEST, preferred_element_type=jnp.float32,
    )


def exchange_order(outer, inner):
    bits = (outer * inner).bit_length() - 1
    core = inner.bit_length() - 1
    return [core] + [b for b in range(bits) if b != core]


def gather_steps(rows, order):
    parts = 1 << len(order)
    gathered = rows[None]

    def from_across(mask):
        return lax.ppermute(gathered, TIME_AXES, [(i, i ^ mask) for i in range(parts)])

    stages = []
    for bits in [order[:1]] + [order[i : i + 2] for i in range(1, len(order), 2)]:
        masks = [0]
        for bit in bits:
            masks += [m | 1 << bit for m in masks]
        gathered = jnp.concatenate([gathered] + [from_across(m) for m in masks[1:]], 0)
        stages.append(gathered)
    return stages


def prepare(
    after_ref, map_ref, var_ref, trans_ref, noise_ref, mean_ref, prior_ref,
    start_ref, turned_ref, chosen_ref, inv_var_ref, trans_out, noise_out, mean_out, prior_out,
):
    size = trans_ref.shape[0]
    sensors = map_ref.shape[1]
    trans = trans_ref[...]
    turned = trans.T
    turned_ref[...] = turned
    rows = jnp.concatenate(
        [trans * prior_ref[...], jnp.broadcast_to(mean_ref[...], (8, size))], 0
    )
    rows = dot3(rows, turned)
    start_ref[:size] = rows[:size] + noise_ref[...]
    start_ref[size:] = rows[size:]
    components = lax.broadcasted_iota(jnp.int32, (size, sensors), 0)
    chosen = (components == map_ref[...]).astype(jnp.float32)
    chosen_ref[...] = chosen.T
    inv_var_ref[...] = 1.0 / var_ref[...]
    trans_out[...] = trans
    noise_out[...] = noise_ref[...]
    mean_out[...] = mean_ref[...]
    prior_out[...] = prior_ref[...]


def kernel(
    own_ref, steps_ref, start_ref, turned_ref, chosen_ref, inv_var_ref, trans_ref, noise_ref,
    mean_ref, prior_ref, mean_out, cov_out, prec_ref, info_ref, state_ref, check_ref, high_ref,
    low_ref, *, order,
):
    parts, rows_each, width = steps_ref.shape
    per_part = rows_each // 2
    steps = parts * per_part
    size = trans_ref.shape[0]
    own = own_ref[0]
    first = own * per_part
    row_ids = lax.broadcasted_iota(jnp.int32, (size, size), 0)
    col_ids = lax.broadcasted_iota(jnp.int32, (size, size), 1)
    on_diag = row_ids == col_ids

    inv_var = inv_var_ref[...]

    def place(source, carried):
        mask = source ^ own
        slot = sum(((mask >> bit) & 1) << i for i, bit in enumerate(order))
        block = steps_ref[slot]
        weight = block[per_part:] * inv_var
        prec_ref[pl.ds(source * per_part, per_part), :] = weight
        info_ref[pl.ds(source * per_part, per_part), :] = weight * block[:per_part]
        return carried

    lax.fori_loop(0, parts, place, 0, unroll=parts <= 8)
    chosen = chosen_ref[...].astype(jnp.bfloat16)
    left = jnp.concatenate([prec_ref[...], info_ref[...]], 0)
    summed = jnp.zeros(left.shape, jnp.float32)
    for _ in range(3):
        part = left.astype(jnp.bfloat16)
        left = left - part.astype(jnp.float32)
        summed = summed + jnp.dot(part, chosen, preferred_element_type=jnp.float32)
    prec_ref[...] = summed[:steps]
    info_ref[...] = summed[steps:]
    high_ref[...], low_ref[...] = split(turned_ref[...])
    check_ref[...] = jnp.zeros_like(check_ref)

    def factors(cov, mean, step):
        prec = prec_ref[pl.ds(step, 1), :]
        info = info_ref[pl.ds(step, 1), :]
        own_var = jnp.sum(jnp.where(on_diag, cov, 0.0), axis=0, keepdims=True)
        shrink = 1.0 / (1.0 + own_var * prec)
        series = jnp.where(on_diag, 0.0, cov * (prec * shrink))
        push = (info - prec * mean) * shrink
        return shrink, series, push

    square, wide, narrow = series_factors()
    whole = 1.0 / (square * wide[1] * narrow[1])

    def advance(cov, mean, step, move, outs):
        shrink, series, push = factors(cov, mean, step)
        series = split(series)
        pow2 = mul(series, series)
        lefts = []
        rights = []
        if move:
            lefts.append(trans_ref[...] * (shrink * whole))
            moved = mul(split(jnp.concatenate([cov, mean], 0)), (high_ref[...], low_ref[...]))
            rights.append(moved[:size])
        if outs:
            lefts.append(jnp.where(on_diag, jnp.broadcast_to(shrink * whole, (size, size)), 0.0))
            rights.append(cov)
        lefts[-1] = jnp.concatenate([lefts[-1], push * whole], 0)
        pow2_split = split(pow2)
        pow4 = jnp.dot(pow2_split[0], pow2_split[0], preferred_element_type=jnp.float32)
        check_ref[step] = jnp.sum((pow4 * pow4).reshape(size // 8, 8, size), axis=0)
        even_left = split(pow4 + pow2 * wide[0])
        even_right = split(pow4 + pow2 * narrow[0])
        done = []
        for left in lefts:
            left = left - mul(split(left), series)
            left = left * square + mul(split(left), pow2_split)
            done.append(split(left * wide[1] + mul(split(left), even_left)))
        rights = [split(right * narrow[1] + mul(even_right, split(right))) for right in rights]
        result = []
        if move:
            final = mul(done[0], rights[0])
            mean_next = final[size:] if not outs else mul(tuple(x[size:] for x in done[1]), rights[0])
            result += [final[:size] + noise_ref[...], mean_next + moved[size:]]
        if outs:
            final = mul(done[-1], rights[-1])
            result += [final[:size], final[size:] + mean]
        return result

    cov, mean = start_ref[:size], start_ref[size:]

    def body(step, carried):
        return tuple(advance(*carried, step, True, False))

    cov, mean = lax.fori_loop(0, first, body, (cov, mean))
    for j in range(per_part):
        moves = j + 1 < per_part
        result = advance(cov, mean, first + j, moves, True)
        if moves:
            cov, mean = result[:2]
        filt_cov, filt_mean = result[-2:]
        cov_out[j] = 0.5 * (filt_cov + filt_cov.T)
        mean_out[pl.ds(j, 1), :] = filt_mean[:1]

    sizes = jnp.sum(jnp.sum(check_ref[...], axis=1), axis=1, keepdims=True)
    failed = jnp.sum(jnp.where(sizes <= SERIES_BOUND, 0.0, 1.0))

    @pl.when(failed > 0.0)
    def _():
        lane = lax.broadcasted_iota(jnp.int32, (1, size), 1)

        def absorb(step, mean):
            prec = prec_ref[pl.ds(step, 1), :]
            info = info_ref[pl.ds(step, 1), :]

            def one(s, mean):
                here = lane == s

                def at(row):
                    return jnp.sum(jnp.where(here, row, 0.0), axis=1, keepdims=True)

                cov = state_ref[...]
                row = state_ref[pl.ds(s, 1), :]
                col = jnp.sum(jnp.where(here, cov, 0.0), axis=1, keepdims=True)
                scale = 1.0 / (1.0 + at(prec) * at(row))
                state_ref[...] = cov - col * (row * (at(prec) * scale))
                return mean + row * ((at(info) - at(prec) * at(mean)) * scale)

            mean = lax.fori_loop(0, size, one, mean)
            cov = state_ref[...]
            state_ref[...] = 0.5 * (cov + cov.T)
            return mean

        def predict(mean):
            cov = dot_full(dot_full(trans_ref[...], state_ref[...]), turned_ref[...])
            state_ref[...] = cov + noise_ref[...]
            return dot_full(jnp.broadcast_to(mean, (8, size)), turned_ref[...])[:1]

        state_ref[...] = dot_full(trans_ref[...] * prior_ref[...], turned_ref[...]) + noise_ref[...]
        mean = dot_full(jnp.broadcast_to(mean_ref[...], (8, size)), turned_ref[...])[:1]
        mean = lax.fori_loop(0, first, lambda t, m: predict(absorb(t, m)), mean)
        for j in range(per_part):
            mean = absorb(first + j, mean)
            cov_out[j] = state_ref[...]
            mean_out[pl.ds(j, 1), :] = mean
            if j + 1 < per_part:
                mean = predict(mean)


def local(
    observations, obs_mask, sensor_map, transition, proc_noise, obs_var, prior_mean, prior_var
):
    steps_here, sensors = observations.shape
    size = transition.shape[0]
    parts = lax.axis_size("outer") * lax.axis_size("inner")
    order = exchange_order(lax.axis_size("outer"), lax.axis_size("inner"))
    position = lax.axis_index("outer") * lax.axis_size("inner") + lax.axis_index("inner")
    rows = jnp.concatenate([observations, obs_mask.astype(jnp.float32)], 0)
    stages = gather_steps(rows, order)
    gathered = stages[-1]
    steps = parts * steps_here
    vmem = pl.BlockSpec(memory_space=pltpu.VMEM)

    def near(*arrays):
        return [pltpu.with_memory_space_constraint(a, pltpu.VMEM) for a in arrays]

    prepared = pl.pallas_call(
        prepare,
        out_shape=(
            pltpu.VMEM((size + 8, size), jnp.float32),
            pltpu.VMEM((size, size), jnp.float32),
            pltpu.VMEM((sensors, size), jnp.float32),
            pltpu.VMEM((1, sensors), jnp.float32),
            pltpu.VMEM((size, size), jnp.float32),
            pltpu.VMEM((size, size), jnp.float32),
            pltpu.VMEM((1, size), jnp.float32),
            pltpu.VMEM((1, size), jnp.float32),
        ),
        in_specs=[vmem] * 7,
        out_specs=(vmem,) * 8,
        name="prepare_window",
    )(*near(stages[0]), sensor_map[None], obs_var[None], transition, proc_noise, prior_mean[None], prior_var[None])
    return pl.pallas_call(
        functools.partial(kernel, order=order),
        out_shape=(
            jax.ShapeDtypeStruct((steps_here, size), jnp.float32),
            jax.ShapeDtypeStruct((steps_here, size, size), jnp.float32),
        ),
        in_specs=[pl.BlockSpec(memory_space=pltpu.SMEM)] + [vmem] * 9,
        out_specs=(vmem, vmem),
        scratch_shapes=[
            pltpu.VMEM((steps, sensors), jnp.float32),
            pltpu.VMEM((steps, sensors), jnp.float32),
            pltpu.VMEM((size, size), jnp.float32),
            pltpu.VMEM((steps, 8, size), jnp.float32),
            pltpu.VMEM((size, size), jnp.bfloat16),
            pltpu.VMEM((size, size), jnp.bfloat16),
        ],
        name="filter_window",
    )(
        position.astype(jnp.int32)[None], *near(gathered, *prepared)
    )


def solution(mesh):
    return jax.shard_map(
        local,
        mesh=mesh,
        in_specs=(
            P(("region", "outer", "inner"), None),
            P(("region", "outer", "inner"), None),
            P("region"),
            P(),
            P(),
            P(),
            P("region"),
            P("region"),
        ),
        out_specs=(
            P(("region", "outer", "inner"), None),
            P(("region", "outer", "inner"), None, None),
        ),
        check_vma=False,
    )
```

```python
import functools
import math

import jax
import jax.numpy as jnp
from jax import lax
from jax.experimental import pallas as pl
from jax.experimental.pallas import tpu as pltpu
from jax.sharding import PartitionSpec as P

RADIUS = 0.6
SERIES_BOUND = RADIUS**8
TIME_AXES = ("outer", "inner")


def series_factors():
    squeeze = 1.0 - RADIUS**2

    def quartic(k):
        cosine = math.cos(k * math.pi / 6)
        const = cosine**2 + squeeze * math.sin(k * math.pi / 6) ** 2
        return 2.0 * const - 4.0 * cosine**2, const**2

    return squeeze, quartic(2), quartic(1)


def split(value):
    high = value.astype(jnp.bfloat16)
    return high, (value - high.astype(jnp.float32)).astype(jnp.bfloat16)


def mul(left, right):
    size = right[0].shape[1]
    columns = jnp.concatenate(right, 1)
    result = jnp.dot(
        jnp.concatenate(left, 1),
        jnp.concatenate([columns, columns], 0),
        preferred_element_type=jnp.float32,
    )
    return result[:, :size] + result[:, size:]


def dot3(left, right):
    return mul(split(left), split(right))


def dot_full(left, right):
    return lax.dot_general(
        left, right, (((1,), (0,)), ((), ())),
        precision=lax.Precision.HIGHEST, preferred_element_type=jnp.float32,
    )


def exchange_stages(outer, inner):
    core = inner.bit_length() - 1
    others = [b for b in range((outer * inner).bit_length() - 1) if b != core]
    return [(core,)] + [tuple(others[i : i + 2]) for i in range(0, len(others), 2)]


def slot_of(mask, stages):
    slot, place = 0, 0
    for stage in stages:
        bits = [(mask >> b) & 1 for b in stage]
        if len(bits) == 2:
            bits[1] = bits[0] ^ bits[1]
        for bit in bits:
            slot = slot + (bit << place)
            place += 1
    return slot


def gather_steps(own_rows, observations, obs_mask, stages):
    parts = 1 << sum(len(stage) for stage in stages)

    def across(value, mask):
        return lax.ppermute(value, TIME_AXES, [(i, i ^ mask) for i in range(parts)])

    mask = 1 << stages[0][0]
    gathered = jnp.stack(
        [
            own_rows,
            jnp.concatenate(
                [across(observations, mask), across(obs_mask, mask).astype(jnp.float32)], 0
            ),
        ],
        0,
    )
    for stage in stages[1:]:
        masks = [1 << b for b in stage]
        if len(masks) == 2:
            masks = [masks[0] | masks[1], masks[1], masks[0]]
        gathered = jnp.concatenate([gathered] + [across(gathered, m) for m in masks], 0)
    return gathered


def prepare(
    read_ref, mask_ref, map_ref, var_ref, trans_ref, noise_ref, mean_ref, prior_ref,
    start_ref, turned_ref, chosen_ref, inv_var_ref, trans_out, noise_out, mean_out, prior_out, rows_out,
):
    rows_out[...] = jnp.concatenate([read_ref[...], mask_ref[...].astype(jnp.float32)], 0)
    size = trans_ref.shape[0]
    sensors = map_ref.shape[1]
    trans = trans_ref[...]
    turned = trans.T
    turned_ref[...] = turned
    rows = jnp.concatenate(
        [trans * prior_ref[...], jnp.broadcast_to(mean_ref[...], (8, size))], 0
    )
    rows = dot3(rows, turned)
    start_ref[:size] = rows[:size] + noise_ref[...]
    start_ref[size:] = rows[size:]
    components = lax.broadcasted_iota(jnp.int32, (size, sensors), 0)
    chosen = (components == map_ref[...]).astype(jnp.float32)
    chosen_ref[...] = chosen.T
    inv_var_ref[...] = 1.0 / var_ref[...]
    trans_out[...] = trans
    noise_out[...] = noise_ref[...]
    mean_out[...] = mean_ref[...]
    prior_out[...] = prior_ref[...]


def kernel(
    steps_ref, start_ref, turned_ref, chosen_ref, inv_var_ref, trans_ref, noise_ref,
    mean_ref, prior_ref, mean_out, cov_out, prec_ref, info_ref, state_ref, check_ref, high_ref,
    low_ref, *, stages,
):
    parts, rows_each, width = steps_ref.shape
    per_part = rows_each // 2
    steps = parts * per_part
    size = trans_ref.shape[0]
    own = lax.axis_index("outer") * lax.axis_size("inner") + lax.axis_index("inner")
    first = own * per_part
    row_ids = lax.broadcasted_iota(jnp.int32, (size, size), 0)
    col_ids = lax.broadcasted_iota(jnp.int32, (size, size), 1)
    on_diag = row_ids == col_ids

    inv_var = inv_var_ref[...]

    def place(source, carried):
        block = steps_ref[slot_of(source ^ own, stages)]
        weight = block[per_part:] * inv_var
        prec_ref[pl.ds(source * per_part, per_part), :] = weight
        info_ref[pl.ds(source * per_part, per_part), :] = weight * block[:per_part]
        return carried

    lax.fori_loop(0, parts, place, 0, unroll=parts <= 8)
    chosen = chosen_ref[...].astype(jnp.bfloat16)
    left = jnp.concatenate([prec_ref[...], info_ref[...]], 0)
    summed = jnp.zeros(left.shape, jnp.float32)
    for _ in range(3):
        part = left.astype(jnp.bfloat16)
        left = left - part.astype(jnp.float32)
        summed = summed + jnp.dot(part, chosen, preferred_element_type=jnp.float32)
    prec_ref[...] = summed[:steps]
    info_ref[...] = summed[steps:]
    high_ref[...], low_ref[...] = split(turned_ref[...])
    check_ref[...] = jnp.zeros_like(check_ref)

    def factors(cov, mean, step):
        prec = prec_ref[pl.ds(step, 1), :]
        info = info_ref[pl.ds(step, 1), :]
        own_var = jnp.sum(jnp.where(on_diag, cov, 0.0), axis=0, keepdims=True)
        shrink = 1.0 / (1.0 + own_var * prec)
        series = jnp.where(on_diag, 0.0, cov * (prec * shrink))
        push = (info - prec * mean) * shrink
        return shrink, series, push

    square, wide, narrow = series_factors()
    whole = 1.0 / (square * wide[1] * narrow[1])

    def advance(cov, mean, step, move, outs):
        shrink, series, push = factors(cov, mean, step)
        series = split(series)
        pow2 = mul(series, series)
        lefts = []
        rights = []
        if move:
            lefts.append(trans_ref[...] * (shrink * whole))
            moved = mul(split(jnp.concatenate([cov, mean], 0)), (high_ref[...], low_ref[...]))
            rights.append(moved[:size])
        if outs:
            lefts.append(jnp.where(on_diag, jnp.broadcast_to(shrink * whole, (size, size)), 0.0))
            rights.append(cov)
        lefts[-1] = jnp.concatenate([lefts[-1], push * whole], 0)
        pow2_split = split(pow2)
        pow4 = jnp.dot(pow2_split[0], pow2_split[0], preferred_element_type=jnp.float32)
        check_ref[step] = jnp.sum((pow4 * pow4).reshape(size // 8, 8, size), axis=0)
        even_left = split(pow4 + pow2 * wide[0])
        even_right = split(pow4 + pow2 * narrow[0])
        done = []
        for left in lefts:
            left = left - mul(split(left), series)
            left = left * square + mul(split(left), pow2_split)
            done.append(split(left * wide[1] + mul(split(left), even_left)))
        rights = [split(right * narrow[1] + mul(even_right, split(right))) for right in rights]
        result = []
        if move:
            final = mul(done[0], rights[0])
            mean_next = final[size:] if not outs else mul(tuple(x[size:] for x in done[1]), rights[0])
            result += [final[:size] + noise_ref[...], mean_next + moved[size:]]
        if outs:
            final = mul(done[-1], rights[-1])
            result += [final[:size], final[size:] + mean]
        return result

    cov, mean = start_ref[:size], start_ref[size:]

    def body(step, carried):
        return tuple(advance(*carried, step, True, False))

    cov, mean = lax.fori_loop(0, first, body, (cov, mean))
    for j in range(per_part):
        moves = j + 1 < per_part
        result = advance(cov, mean, first + j, moves, True)
        if moves:
            cov, mean = result[:2]
        filt_cov, filt_mean = result[-2:]
        cov_out[j] = 0.5 * (filt_cov + filt_cov.T)
        mean_out[pl.ds(j, 1), :] = filt_mean[:1]

    sizes = jnp.sum(jnp.sum(check_ref[...], axis=1), axis=1, keepdims=True)
    failed = jnp.sum(jnp.where(sizes <= SERIES_BOUND, 0.0, 1.0))

    @pl.when(failed > 0.0)
    def _():
        lane = lax.broadcasted_iota(jnp.int32, (1, size), 1)

        def absorb(step, mean):
            prec = prec_ref[pl.ds(step, 1), :]
            info = info_ref[pl.ds(step, 1), :]

            def one(s, mean):
                here = lane == s

                def at(row):
                    return jnp.sum(jnp.where(here, row, 0.0), axis=1, keepdims=True)

                cov = state_ref[...]
                row = state_ref[pl.ds(s, 1), :]
                col = jnp.sum(jnp.where(here, cov, 0.0), axis=1, keepdims=True)
                scale = 1.0 / (1.0 + at(prec) * at(row))
                state_ref[...] = cov - col * (row * (at(prec) * scale))
                return mean + row * ((at(info) - at(prec) * at(mean)) * scale)

            mean = lax.fori_loop(0, size, one, mean)
            cov = state_ref[...]
            state_ref[...] = 0.5 * (cov + cov.T)
            return mean

        def predict(mean):
            cov = dot_full(dot_full(trans_ref[...], state_ref[...]), turned_ref[...])
            state_ref[...] = cov + noise_ref[...]
            return dot_full(jnp.broadcast_to(mean, (8, size)), turned_ref[...])[:1]

        state_ref[...] = dot_full(trans_ref[...] * prior_ref[...], turned_ref[...]) + noise_ref[...]
        mean = dot_full(jnp.broadcast_to(mean_ref[...], (8, size)), turned_ref[...])[:1]
        mean = lax.fori_loop(0, first, lambda t, m: predict(absorb(t, m)), mean)
        for j in range(per_part):
            mean = absorb(first + j, mean)
            cov_out[j] = state_ref[...]
            mean_out[pl.ds(j, 1), :] = mean
            if j + 1 < per_part:
                mean = predict(mean)


def local(
    observations, obs_mask, sensor_map, transition, proc_noise, obs_var, prior_mean, prior_var
):
    steps_here, sensors = observations.shape
    size = transition.shape[0]
    parts = lax.axis_size("outer") * lax.axis_size("inner")
    stages = exchange_stages(lax.axis_size("outer"), lax.axis_size("inner"))
    steps = parts * steps_here
    vmem = pl.BlockSpec(memory_space=pltpu.VMEM)

    def near(*arrays):
        return [pltpu.with_memory_space_constraint(a, pltpu.VMEM) for a in arrays]

    *prepared, own_rows = pl.pallas_call(
        prepare,
        out_shape=(
            pltpu.VMEM((size + 8, size), jnp.float32),
            pltpu.VMEM((size, size), jnp.float32),
            pltpu.VMEM((sensors, size), jnp.float32),
            pltpu.VMEM((1, sensors), jnp.float32),
            pltpu.VMEM((size, size), jnp.float32),
            pltpu.VMEM((size, size), jnp.float32),
            pltpu.VMEM((1, size), jnp.float32),
            pltpu.VMEM((1, size), jnp.float32),
            pltpu.VMEM((2 * steps_here, sensors), jnp.float32),
        ),
        in_specs=[vmem] * 8,
        out_specs=(vmem,) * 9,
        name="prepare_window",
    )(
        observations, obs_mask, sensor_map[None], obs_var[None], transition, proc_noise,
        prior_mean[None], prior_var[None],
    )
    gathered = gather_steps(own_rows, observations, obs_mask, stages)
    return pl.pallas_call(
        functools.partial(kernel, stages=stages),
        out_shape=(
            jax.ShapeDtypeStruct((steps_here, size), jnp.float32),
            jax.ShapeDtypeStruct((steps_here, size, size), jnp.float32),
        ),
        in_specs=[vmem] * 9,
        out_specs=(vmem, vmem),
        scratch_shapes=[
            pltpu.VMEM((steps, sensors), jnp.float32),
            pltpu.VMEM((steps, sensors), jnp.float32),
            pltpu.VMEM((size, size), jnp.float32),
            pltpu.VMEM((steps, 8, size), jnp.float32),
            pltpu.VMEM((size, size), jnp.bfloat16),
            pltpu.VMEM((size, size), jnp.bfloat16),
        ],
        name="filter_window",
    )(
        *near(gathered, *prepared)
    )


def solution(mesh):
    return jax.shard_map(
        local,
        mesh=mesh,
        in_specs=(
            P(("region", "outer", "inner"), None),
            P(("region", "outer", "inner"), None),
            P("region"),
            P(),
            P(),
            P(),
            P("region"),
            P("region"),
        ),
        out_specs=(
            P(("region", "outer", "inner"), None),
            P(("region", "outer", "inner"), None, None),
        ),
        check_vma=False,
    )
```

```python
import functools
import math

import jax
import jax.numpy as jnp
from jax import lax
from jax.experimental import pallas as pl
from jax.experimental.pallas import tpu as pltpu
from jax.sharding import PartitionSpec as P


RADIUS = 0.6
SERIES_BOUND = RADIUS**8
TIME_AXES = ("outer", "inner")


def series_factors():
    squeeze = 1.0 - RADIUS**2

    def quartic(k):
        cosine = math.cos(k * math.pi / 6)
        const = cosine**2 + squeeze * math.sin(k * math.pi / 6) ** 2
        return 2.0 * const - 4.0 * cosine**2, const**2

    return squeeze, quartic(2), quartic(1)


def split(value):
    high = value.astype(jnp.bfloat16)
    return high, (value - high.astype(jnp.float32)).astype(jnp.bfloat16)


def mul(left, right):
    size = right[0].shape[1]
    columns = jnp.concatenate(right, 1)
    result = jnp.dot(
        jnp.concatenate(left, 1),
        jnp.concatenate([columns, columns], 0),
        preferred_element_type=jnp.float32,
    )
    return result[:, :size] + result[:, size:]


def dot3(left, right):
    return mul(split(left), split(right))


def dot_full(left, right):
    return lax.dot_general(
        left, right, (((1,), (0,)), ((), ())),
        precision=lax.Precision.HIGHEST, preferred_element_type=jnp.float32,
    )


def exchange_stages(outer, inner):
    core = inner.bit_length() - 1
    others = [b for b in range((outer * inner).bit_length() - 1) if b != core]
    return [(core,)] + [tuple(others[i : i + 2]) for i in range(0, len(others), 2)]


def slot_of(mask, stages):
    slot, place = 0, 0
    for stage in stages:
        bits = [(mask >> b) & 1 for b in stage]
        if len(bits) == 2:
            bits[1] = bits[0] ^ bits[1]
        for bit in bits:
            slot = slot + (bit << place)
            place += 1
    return slot


def gather_steps(own_rows, observations, obs_mask, stages):
    parts = 1 << sum(len(stage) for stage in stages)

    def across(value, mask):
        return lax.ppermute(value, TIME_AXES, [(i, i ^ mask) for i in range(parts)])

    mask = 1 << stages[0][0]
    gathered = jnp.stack(
        [
            own_rows,
            jnp.concatenate(
                [across(observations, mask), across(obs_mask, mask).astype(jnp.float32)], 0
            ),
        ],
        0,
    )
    for stage in stages[1:]:
        masks = [1 << b for b in stage]
        if len(masks) == 2:
            masks = [masks[0] | masks[1], masks[1], masks[0]]
        arrived = []
        for m in masks:
            arrived.append(across(gathered, m))
        early = jnp.concatenate([gathered, arrived[0]], 0)
        gathered = jnp.concatenate([gathered] + arrived, 0)
    return early, gathered


def prepare(
    read_ref, mask_ref, map_ref, var_ref, trans_ref, noise_ref, mean_ref, prior_ref,
    start_ref, turned_ref, chosen_ref, inv_var_ref, trans_out, noise_out, mean_out, prior_out, rows_out,
):
    rows_out[...] = jnp.concatenate([read_ref[...], mask_ref[...].astype(jnp.float32)], 0)
    size = trans_ref.shape[0]
    sensors = map_ref.shape[1]
    trans = trans_ref[...]
    turned = trans.T
    turned_ref[...] = turned
    rows = jnp.concatenate(
        [trans * prior_ref[...], jnp.broadcast_to(mean_ref[...], (8, size))], 0
    )
    rows = dot3(rows, turned)
    start_ref[:size] = rows[:size] + noise_ref[...]
    start_ref[size:] = rows[size:]
    components = lax.broadcasted_iota(jnp.int32, (size, sensors), 0)
    chosen = (components == map_ref[...]).astype(jnp.float32)
    chosen_ref[...] = chosen.T
    inv_var_ref[...] = 1.0 / var_ref[...]
    trans_out[...] = trans
    noise_out[...] = noise_ref[...]
    mean_out[...] = mean_ref[...]
    prior_out[...] = prior_ref[...]


def kernel(
    steps_ref, start_ref, turned_ref, chosen_ref, inv_var_ref, trans_ref, noise_ref,
    mean_ref, prior_ref, tested_ref, mean_out, cov_out, prec_ref, info_ref, state_ref, check_ref,
    high_ref, low_ref, *, stages, known, early,
):
    rows_each = steps_ref.shape[1]
    parts = 1 << sum(len(stage) for stage in stages)
    per_part = rows_each // 2
    steps = parts * per_part
    size = trans_ref.shape[0]
    own = lax.axis_index("outer") * lax.axis_size("inner") + lax.axis_index("inner")
    first = own * per_part
    row_ids = lax.broadcasted_iota(jnp.int32, (size, size), 0)
    col_ids = lax.broadcasted_iota(jnp.int32, (size, size), 1)
    on_diag = row_ids == col_ids

    inv_var = inv_var_ref[...]

    head_slot = slot_of(own, stages)
    has_head = jnp.logical_and(head_slot < known, own > 0)
    headway = jnp.where(has_head, per_part, 0)

    def place(source, carried):
        if early:
            block = steps_ref[jnp.where(has_head, head_slot, 0)]
        else:
            block = steps_ref[slot_of(source ^ own, stages)]
        weight = block[per_part:] * inv_var
        prec_ref[pl.ds(source * per_part, per_part), :] = weight
        info_ref[pl.ds(source * per_part, per_part), :] = weight * block[:per_part]
        return carried

    if early:
        prec_ref[...] = jnp.zeros_like(prec_ref)
        info_ref[...] = jnp.zeros_like(info_ref)
        place(0, 0)
    else:
        lax.fori_loop(0, parts, place, 0, unroll=parts <= 8)
    chosen = chosen_ref[...].astype(jnp.bfloat16)
    left = jnp.concatenate([prec_ref[...], info_ref[...]], 0)
    summed = jnp.zeros(left.shape, jnp.float32)
    for _ in range(3):
        part = left.astype(jnp.bfloat16)
        left = left - part.astype(jnp.float32)
        summed = summed + jnp.dot(part, chosen, preferred_element_type=jnp.float32)
    prec_ref[...] = summed[:steps]
    info_ref[...] = summed[steps:]
    high_ref[...], low_ref[...] = split(turned_ref[...])
    check_ref[...] = jnp.zeros_like(check_ref)
    if not early:
        check_ref[:per_part] = tested_ref[...]

    def factors(cov, mean, step):
        prec = prec_ref[pl.ds(step, 1), :]
        info = info_ref[pl.ds(step, 1), :]
        own_var = jnp.sum(jnp.where(on_diag, cov, 0.0), axis=0, keepdims=True)
        shrink = 1.0 / (1.0 + own_var * prec)
        series = jnp.where(on_diag, 0.0, cov * (prec * shrink))
        push = (info - prec * mean) * shrink
        return shrink, series, push

    square, wide, narrow = series_factors()
    whole = 1.0 / (square * wide[1] * narrow[1])

    def advance(cov, mean, step, move, outs):
        shrink, series, push = factors(cov, mean, step)
        series = split(series)
        pow2 = mul(series, series)
        lefts = []
        rights = []
        if move:
            lefts.append(trans_ref[...] * (shrink * whole))
            moved = mul(split(jnp.concatenate([cov, mean], 0)), (high_ref[...], low_ref[...]))
            rights.append(moved[:size])
        if outs:
            lefts.append(jnp.where(on_diag, jnp.broadcast_to(shrink * whole, (size, size)), 0.0))
            rights.append(cov)
        lefts[-1] = jnp.concatenate([lefts[-1], push * whole], 0)
        pow2_split = split(pow2)
        pow4 = jnp.dot(pow2_split[0], pow2_split[0], preferred_element_type=jnp.float32)
        check_ref[step] = jnp.sum((pow4 * pow4).reshape(size // 8, 8, size), axis=0)
        even_left = split(pow4 + pow2 * wide[0])
        even_right = split(pow4 + pow2 * narrow[0])
        done = []
        for left in lefts:
            left = left - mul(split(left), series)
            left = left * square + mul(split(left), pow2_split)
            done.append(split(left * wide[1] + mul(split(left), even_left)))
        rights = [split(right * narrow[1] + mul(even_right, split(right))) for right in rights]
        result = []
        if move:
            final = mul(done[0], rights[0])
            mean_next = final[size:] if not outs else mul(tuple(x[size:] for x in done[1]), rights[0])
            result += [final[:size] + noise_ref[...], mean_next + moved[size:]]
        if outs:
            final = mul(done[-1], rights[-1])
            result += [final[:size], final[size:] + mean]
        return result

    cov, mean = start_ref[:size], start_ref[size:]

    def body(step, carried):
        return tuple(advance(*carried, step, True, False))

    if early:
        cov, mean = lax.fori_loop(0, headway, body, (cov, mean))
        mean_out[:size] = cov
        mean_out[size:] = mean
        cov_out[...] = check_ref[:per_part]
        return
    cov, mean = lax.fori_loop(headway, first, body, (cov, mean))
    for j in range(per_part):
        moves = j + 1 < per_part
        result = advance(cov, mean, first + j, moves, True)
        if moves:
            cov, mean = result[:2]
        filt_cov, filt_mean = result[-2:]
        cov_out[j] = 0.5 * (filt_cov + filt_cov.T)
        mean_out[pl.ds(j, 1), :] = filt_mean[:1]

    sizes = jnp.sum(jnp.sum(check_ref[...], axis=1), axis=1, keepdims=True)
    failed = jnp.sum(jnp.where(sizes <= SERIES_BOUND, 0.0, 1.0))

    @pl.when(failed > 0.0)
    def _():
        lane = lax.broadcasted_iota(jnp.int32, (1, size), 1)

        def absorb(step, mean):
            prec = prec_ref[pl.ds(step, 1), :]
            info = info_ref[pl.ds(step, 1), :]

            def one(s, mean):
                here = lane == s

                def at(row):
                    return jnp.sum(jnp.where(here, row, 0.0), axis=1, keepdims=True)

                cov = state_ref[...]
                row = state_ref[pl.ds(s, 1), :]
                col = jnp.sum(jnp.where(here, cov, 0.0), axis=1, keepdims=True)
                scale = 1.0 / (1.0 + at(prec) * at(row))
                state_ref[...] = cov - col * (row * (at(prec) * scale))
                return mean + row * ((at(info) - at(prec) * at(mean)) * scale)

            mean = lax.fori_loop(0, size, one, mean)
            cov = state_ref[...]
            state_ref[...] = 0.5 * (cov + cov.T)
            return mean

        def predict(mean):
            cov = dot_full(dot_full(trans_ref[...], state_ref[...]), turned_ref[...])
            state_ref[...] = cov + noise_ref[...]
            return dot_full(jnp.broadcast_to(mean, (8, size)), turned_ref[...])[:1]

        state_ref[...] = dot_full(trans_ref[...] * prior_ref[...], turned_ref[...]) + noise_ref[...]
        mean = dot_full(jnp.broadcast_to(mean_ref[...], (8, size)), turned_ref[...])[:1]
        mean = lax.fori_loop(0, first, lambda t, m: predict(absorb(t, m)), mean)
        for j in range(per_part):
            mean = absorb(first + j, mean)
            cov_out[j] = state_ref[...]
            mean_out[pl.ds(j, 1), :] = mean
            if j + 1 < per_part:
                mean = predict(mean)


def local(
    observations, obs_mask, sensor_map, transition, proc_noise, obs_var, prior_mean, prior_var
):
    steps_here, sensors = observations.shape
    size = transition.shape[0]
    parts = lax.axis_size("outer") * lax.axis_size("inner")
    stages = exchange_stages(lax.axis_size("outer"), lax.axis_size("inner"))
    steps = parts * steps_here
    vmem = pl.BlockSpec(memory_space=pltpu.VMEM)

    def near(*arrays):
        return [pltpu.with_memory_space_constraint(a, pltpu.VMEM) for a in arrays]

    *prepared, own_rows = pl.pallas_call(
        prepare,
        out_shape=(
            pltpu.VMEM((size + 8, size), jnp.float32),
            pltpu.VMEM((size, size), jnp.float32),
            pltpu.VMEM((sensors, size), jnp.float32),
            pltpu.VMEM((1, sensors), jnp.float32),
            pltpu.VMEM((size, size), jnp.float32),
            pltpu.VMEM((size, size), jnp.float32),
            pltpu.VMEM((1, size), jnp.float32),
            pltpu.VMEM((1, size), jnp.float32),
            pltpu.VMEM((2 * steps_here, sensors), jnp.float32),
        ),
        in_specs=[vmem] * 8,
        out_specs=(vmem,) * 9,
        name="prepare_window",
    )(
        observations, obs_mask, sensor_map[None], obs_var[None], transition, proc_noise,
        prior_mean[None], prior_var[None],
    )
    early, gathered = gather_steps(own_rows, observations, obs_mask, stages)
    scratch = [
        pltpu.VMEM((steps, sensors), jnp.float32),
        pltpu.VMEM((steps, sensors), jnp.float32),
        pltpu.VMEM((size, size), jnp.float32),
        pltpu.VMEM((steps, 8, size), jnp.float32),
        pltpu.VMEM((size, size), jnp.bfloat16),
        pltpu.VMEM((size, size), jnp.bfloat16),
    ]
    known = early.shape[0]
    untested = pltpu.VMEM((steps_here, 8, size), jnp.float32)

    def head(*refs):
        kernel(*refs[:9], None, *refs[9:], stages=stages, known=known, early=True)

    state, tested = pl.pallas_call(
        head,
        out_shape=(pltpu.VMEM((size + 8, size), jnp.float32), untested),
        in_specs=[vmem] * 9,
        out_specs=(vmem, vmem),
        scratch_shapes=scratch,
        name="filter_head",
    )(*near(early, *prepared))
    return pl.pallas_call(
        functools.partial(kernel, stages=stages, known=known, early=False),
        out_shape=(
            jax.ShapeDtypeStruct((steps_here, size), jnp.float32),
            jax.ShapeDtypeStruct((steps_here, size, size), jnp.float32),
        ),
        in_specs=[vmem] * 10,
        out_specs=(vmem, vmem),
        scratch_shapes=scratch,
        name="filter_window",
    )(*near(gathered, state, *prepared[1:], tested))


def solution(mesh):
    return jax.shard_map(
        local,
        mesh=mesh,
        in_specs=(
            P(("region", "outer", "inner"), None),
            P(("region", "outer", "inner"), None),
            P("region"),
            P(),
            P(),
            P(),
            P("region"),
            P("region"),
        ),
        out_specs=(
            P(("region", "outer", "inner"), None),
            P(("region", "outer", "inner"), None, None),
        ),
        check_vma=False,
    )
```

```python
import functools
import math

import jax
import jax.numpy as jnp
from jax import lax
from jax.experimental import pallas as pl
from jax.experimental.pallas import tpu as pltpu
from jax.sharding import PartitionSpec as P


RADIUS = 0.6
SERIES_BOUND = RADIUS**8
TIME_AXES = ("outer", "inner")


def series_factors():
    squeeze = 1.0 - RADIUS**2

    def quartic(k):
        cosine = math.cos(k * math.pi / 6)
        const = cosine**2 + squeeze * math.sin(k * math.pi / 6) ** 2
        return 2.0 * const - 4.0 * cosine**2, const**2

    return squeeze, quartic(2), quartic(1)


def split(value):
    high = value.astype(jnp.bfloat16)
    return high, (value - high.astype(jnp.float32)).astype(jnp.bfloat16)


def mul(left, right):
    size = right[0].shape[1]
    columns = jnp.concatenate(right, 1)
    result = jnp.dot(
        jnp.concatenate(left, 1),
        jnp.concatenate([columns, columns], 0),
        preferred_element_type=jnp.float32,
    )
    return result[:, :size] + result[:, size:]


def dot3(left, right):
    return mul(split(left), split(right))


def dot_full(left, right):
    return lax.dot_general(
        left, right, (((1,), (0,)), ((), ())),
        precision=lax.Precision.HIGHEST, preferred_element_type=jnp.float32,
    )


def exchange_stages(outer, inner):
    core = inner.bit_length() - 1
    others = [b for b in range((outer * inner).bit_length() - 1) if b != core]
    return [(core,)] + [tuple(others[i : i + 2]) for i in range(0, len(others), 2)]


def slot_of(mask, stages):
    slot, place = 0, 0
    for stage in stages:
        bits = [(mask >> b) & 1 for b in stage]
        if len(bits) == 2:
            bits[1] = bits[0] ^ bits[1]
        for bit in bits:
            slot = slot + (bit << place)
            place += 1
    return slot


def gather_steps(own_rows, observations, obs_mask, stages):
    parts = 1 << sum(len(stage) for stage in stages)

    def across(value, mask):
        return lax.ppermute(value, TIME_AXES, [(i, i ^ mask) for i in range(parts)])

    mask = 1 << stages[0][0]
    gathered = jnp.stack(
        [
            own_rows,
            jnp.concatenate(
                [across(observations, mask), across(obs_mask, mask).astype(jnp.float32)], 0
            ),
        ],
        0,
    )
    for stage in stages[1:]:
        masks = [1 << b for b in stage]
        if len(masks) == 2:
            masks = [masks[0] | masks[1], masks[1], masks[0]]
        arrived = []
        for m in masks:
            arrived.append(across(gathered, m))
        early = jnp.concatenate([gathered, arrived[0]], 0)
        gathered = jnp.concatenate([gathered] + arrived, 0)
    return early, gathered


def prepare(
    read_ref, mask_ref, map_ref, var_ref, trans_ref, noise_ref, mean_ref, prior_ref,
    start_ref, turned_ref, chosen_ref, inv_var_ref, trans_out, noise_out, mean_out, prior_out, rows_out,
):
    rows_out[...] = jnp.concatenate([read_ref[...], mask_ref[...].astype(jnp.float32)], 0)
    size = trans_ref.shape[0]
    sensors = map_ref.shape[1]
    trans = trans_ref[...]
    turned = trans.T
    turned_ref[...] = turned
    rows = jnp.concatenate(
        [trans * prior_ref[...], jnp.broadcast_to(mean_ref[...], (8, size))], 0
    )
    rows = dot3(rows, turned)
    start_ref[:size] = rows[:size] + noise_ref[...]
    start_ref[size:] = rows[size:]
    components = lax.broadcasted_iota(jnp.int32, (size, sensors), 0)
    chosen = (components == map_ref[...]).astype(jnp.float32)
    chosen_ref[...] = chosen.T
    inv_var_ref[...] = 1.0 / var_ref[...]
    trans_out[...] = trans
    noise_out[...] = noise_ref[...]
    mean_out[...] = mean_ref[...]
    prior_out[...] = prior_ref[...]


def kernel(
    steps_ref, start_ref, turned_ref, chosen_ref, inv_var_ref, trans_ref, noise_ref,
    mean_ref, prior_ref, tested_ref, mean_out, cov_out, prec_ref, info_ref, state_ref, check_ref,
    high_ref, low_ref, *, stages, known, early,
):
    rows_each = steps_ref.shape[1]
    parts = 1 << sum(len(stage) for stage in stages)
    per_part = rows_each // 2
    steps = parts * per_part
    size = trans_ref.shape[0]
    own = lax.axis_index("outer") * lax.axis_size("inner") + lax.axis_index("inner")
    first = own * per_part
    row_ids = lax.broadcasted_iota(jnp.int32, (size, size), 0)
    col_ids = lax.broadcasted_iota(jnp.int32, (size, size), 1)
    on_diag = row_ids == col_ids

    inv_var = inv_var_ref[...]

    head_slot = slot_of(own, stages)
    has_head = jnp.logical_and(head_slot < known, own > 0)
    headway = jnp.where(has_head, per_part, 0)

    def place(source, carried):
        if early:
            block = steps_ref[jnp.where(has_head, head_slot, 0)]
        else:
            block = steps_ref[slot_of(source ^ own, stages)]
        weight = block[per_part:] * inv_var
        prec_ref[pl.ds(source * per_part, per_part), :] = weight
        info_ref[pl.ds(source * per_part, per_part), :] = weight * block[:per_part]
        return carried

    if early:
        prec_ref[...] = jnp.zeros_like(prec_ref)
        info_ref[...] = jnp.zeros_like(info_ref)
        place(0, 0)
    else:
        lax.fori_loop(0, parts, place, 0, unroll=parts <= 8)
    chosen = chosen_ref[...].astype(jnp.bfloat16)
    left = jnp.concatenate([prec_ref[...], info_ref[...]], 0)
    summed = jnp.zeros(left.shape, jnp.float32)
    for _ in range(3):
        part = left.astype(jnp.bfloat16)
        left = left - part.astype(jnp.float32)
        summed = summed + jnp.dot(part, chosen, preferred_element_type=jnp.float32)
    prec_ref[...] = summed[:steps]
    info_ref[...] = summed[steps:]
    high_ref[...], low_ref[...] = split(turned_ref[...])
    check_ref[...] = jnp.zeros_like(check_ref)
    if not early:
        check_ref[:per_part] = tested_ref[...]

    def factors(cov, mean, step):
        prec = prec_ref[pl.ds(step, 1), :]
        info = info_ref[pl.ds(step, 1), :]
        own_var = jnp.sum(jnp.where(on_diag, cov, 0.0), axis=0, keepdims=True)
        shrink = 1.0 / (1.0 + own_var * prec)
        series = jnp.where(on_diag, 0.0, cov * (prec * shrink))
        push = (info - prec * mean) * shrink
        return shrink, series, push

    square, wide, narrow = series_factors()
    whole = 1.0 / (square * wide[1] * narrow[1])

    def advance(cov, mean, step, move, outs):
        shrink, series, push = factors(cov, mean, step)
        whole_series = series
        series = split(series)
        lefts = []
        rights = []
        if move:
            lefts.append(trans_ref[...] * (shrink * whole))
            moved = mul(split(jnp.concatenate([cov, mean], 0)), (high_ref[...], low_ref[...]))
            rights.append(moved[:size])
        if outs:
            lefts.append(jnp.where(on_diag, jnp.broadcast_to(shrink * whole, (size, size)), 0.0))
            rights.append(cov)
        lefts[-1] = jnp.concatenate([lefts[-1], push * whole], 0)
        stacked = mul(split(jnp.concatenate([whole_series] + lefts, 0)), series)
        pow2 = stacked[:size]
        lowered = [stacked[size:]]
        if len(lefts) == 2:
            lowered = [stacked[size : 2 * size], stacked[2 * size :]]
        lefts = [left - low for left, low in zip(lefts, lowered)]
        pow2_split = split(pow2)
        pow4 = jnp.dot(pow2_split[0], pow2_split[0], preferred_element_type=jnp.float32)
        check_ref[step] = jnp.sum((pow4 * pow4).reshape(size // 8, 8, size), axis=0)
        even_left = split(pow4 + pow2 * wide[0])
        even_right = split(pow4 + pow2 * narrow[0])
        done = []
        for left in lefts:
            left = left * square + mul(split(left), pow2_split)
            done.append(split(left * wide[1] + mul(split(left), even_left)))
        rights = [split(right * narrow[1] + mul(even_right, split(right))) for right in rights]
        result = []
        if move:
            final = mul(done[0], rights[0])
            mean_next = final[size:] if not outs else mul(tuple(x[size:] for x in done[1]), rights[0])
            result += [final[:size] + noise_ref[...], mean_next + moved[size:]]
        if outs:
            final = mul(done[-1], rights[-1])
            result += [final[:size], final[size:] + mean]
        return result

    cov, mean = start_ref[:size], start_ref[size:]

    def body(step, carried):
        return tuple(advance(*carried, step, True, False))

    if early:
        cov, mean = lax.fori_loop(0, headway, body, (cov, mean))
        mean_out[:size] = cov
        mean_out[size:] = mean
        cov_out[...] = check_ref[:per_part]
        return
    cov, mean = lax.fori_loop(headway, first, body, (cov, mean))
    for j in range(per_part):
        moves = j + 1 < per_part
        result = advance(cov, mean, first + j, moves, True)
        if moves:
            cov, mean = result[:2]
        filt_cov, filt_mean = result[-2:]
        cov_out[j] = 0.5 * (filt_cov + filt_cov.T)
        mean_out[pl.ds(j, 1), :] = filt_mean[:1]

    sizes = jnp.sum(jnp.sum(check_ref[...], axis=1), axis=1, keepdims=True)
    failed = jnp.sum(jnp.where(sizes <= SERIES_BOUND, 0.0, 1.0))

    @pl.when(failed > 0.0)
    def _():
        lane = lax.broadcasted_iota(jnp.int32, (1, size), 1)

        def absorb(step, mean):
            prec = prec_ref[pl.ds(step, 1), :]
            info = info_ref[pl.ds(step, 1), :]

            def one(s, mean):
                here = lane == s

                def at(row):
                    return jnp.sum(jnp.where(here, row, 0.0), axis=1, keepdims=True)

                cov = state_ref[...]
                row = state_ref[pl.ds(s, 1), :]
                col = jnp.sum(jnp.where(here, cov, 0.0), axis=1, keepdims=True)
                scale = 1.0 / (1.0 + at(prec) * at(row))
                state_ref[...] = cov - col * (row * (at(prec) * scale))
                return mean + row * ((at(info) - at(prec) * at(mean)) * scale)

            mean = lax.fori_loop(0, size, one, mean)
            cov = state_ref[...]
            state_ref[...] = 0.5 * (cov + cov.T)
            return mean

        def predict(mean):
            cov = dot_full(dot_full(trans_ref[...], state_ref[...]), turned_ref[...])
            state_ref[...] = cov + noise_ref[...]
            return dot_full(jnp.broadcast_to(mean, (8, size)), turned_ref[...])[:1]

        state_ref[...] = dot_full(trans_ref[...] * prior_ref[...], turned_ref[...]) + noise_ref[...]
        mean = dot_full(jnp.broadcast_to(mean_ref[...], (8, size)), turned_ref[...])[:1]
        mean = lax.fori_loop(0, first, lambda t, m: predict(absorb(t, m)), mean)
        for j in range(per_part):
            mean = absorb(first + j, mean)
            cov_out[j] = state_ref[...]
            mean_out[pl.ds(j, 1), :] = mean
            if j + 1 < per_part:
                mean = predict(mean)


def local(
    observations, obs_mask, sensor_map, transition, proc_noise, obs_var, prior_mean, prior_var
):
    steps_here, sensors = observations.shape
    size = transition.shape[0]
    parts = lax.axis_size("outer") * lax.axis_size("inner")
    stages = exchange_stages(lax.axis_size("outer"), lax.axis_size("inner"))
    steps = parts * steps_here
    vmem = pl.BlockSpec(memory_space=pltpu.VMEM)

    def near(*arrays):
        return [pltpu.with_memory_space_constraint(a, pltpu.VMEM) for a in arrays]

    *prepared, own_rows = pl.pallas_call(
        prepare,
        out_shape=(
            pltpu.VMEM((size + 8, size), jnp.float32),
            pltpu.VMEM((size, size), jnp.float32),
            pltpu.VMEM((sensors, size), jnp.float32),
            pltpu.VMEM((1, sensors), jnp.float32),
            pltpu.VMEM((size, size), jnp.float32),
            pltpu.VMEM((size, size), jnp.float32),
            pltpu.VMEM((1, size), jnp.float32),
            pltpu.VMEM((1, size), jnp.float32),
            pltpu.VMEM((2 * steps_here, sensors), jnp.float32),
        ),
        in_specs=[vmem] * 8,
        out_specs=(vmem,) * 9,
        name="prepare_window",
    )(
        observations, obs_mask, sensor_map[None], obs_var[None], transition, proc_noise,
        prior_mean[None], prior_var[None],
    )
    early, gathered = gather_steps(own_rows, observations, obs_mask, stages)
    scratch = [
        pltpu.VMEM((steps, sensors), jnp.float32),
        pltpu.VMEM((steps, sensors), jnp.float32),
        pltpu.VMEM((size, size), jnp.float32),
        pltpu.VMEM((steps, 8, size), jnp.float32),
        pltpu.VMEM((size, size), jnp.bfloat16),
        pltpu.VMEM((size, size), jnp.bfloat16),
    ]
    known = early.shape[0]
    untested = pltpu.VMEM((steps_here, 8, size), jnp.float32)

    def head(*refs):
        kernel(*refs[:9], None, *refs[9:], stages=stages, known=known, early=True)

    state, tested = pl.pallas_call(
        head,
        out_shape=(pltpu.VMEM((size + 8, size), jnp.float32), untested),
        in_specs=[vmem] * 9,
        out_specs=(vmem, vmem),
        scratch_shapes=scratch,
        name="filter_head",
    )(*near(early, *prepared))
    return pl.pallas_call(
        functools.partial(kernel, stages=stages, known=known, early=False),
        out_shape=(
            jax.ShapeDtypeStruct((steps_here, size), jnp.float32),
            jax.ShapeDtypeStruct((steps_here, size, size), jnp.float32),
        ),
        in_specs=[vmem] * 10,
        out_specs=(vmem, vmem),
        scratch_shapes=scratch,
        name="filter_window",
    )(*near(gathered, state, *prepared[1:], tested))


def solution(mesh):
    return jax.shard_map(
        local,
        mesh=mesh,
        in_specs=(
            P(("region", "outer", "inner"), None),
            P(("region", "outer", "inner"), None),
            P("region"),
            P(),
            P(),
            P(),
            P("region"),
            P("region"),
        ),
        out_specs=(
            P(("region", "outer", "inner"), None),
            P(("region", "outer", "inner"), None, None),
        ),
        check_vma=False,
    )
```

```python
import functools
import math

import jax
import jax.numpy as jnp
from jax import lax
from jax.experimental import pallas as pl
from jax.experimental.pallas import tpu as pltpu
from jax.sharding import PartitionSpec as P


RADIUS = 0.6
SERIES_BOUND = RADIUS**8
TIME_AXES = ("outer", "inner")


def series_factors():
    squeeze = 1.0 - RADIUS**2

    def quartic(k):
        cosine = math.cos(k * math.pi / 6)
        const = cosine**2 + squeeze * math.sin(k * math.pi / 6) ** 2
        return 2.0 * const - 4.0 * cosine**2, const**2

    return squeeze, quartic(2), quartic(1)


def split(value):
    high = value.astype(jnp.bfloat16)
    return high, (value - high.astype(jnp.float32)).astype(jnp.bfloat16)


def mul(left, right):
    size = right[0].shape[1]
    columns = jnp.concatenate(right, 1)
    result = jnp.dot(
        jnp.concatenate(left, 1),
        jnp.concatenate([columns, columns], 0),
        preferred_element_type=jnp.float32,
    )
    return result[:, :size] + result[:, size:]


def dot3(left, right):
    return mul(split(left), split(right))


def dot_full(left, right):
    return lax.dot_general(
        left, right, (((1,), (0,)), ((), ())),
        precision=lax.Precision.HIGHEST, preferred_element_type=jnp.float32,
    )


def exchange_stages(outer, inner):
    core = inner.bit_length() - 1
    others = [b for b in range((outer * inner).bit_length() - 1) if b != core]
    return [(core,)] + [tuple(others[i : i + 2]) for i in range(0, len(others), 2)]


def slot_of(mask, stages):
    slot, place = 0, 0
    for stage in stages:
        bits = [(mask >> b) & 1 for b in stage]
        if len(bits) == 2:
            bits[1] = bits[0] ^ bits[1]
        for bit in bits:
            slot = slot + (bit << place)
            place += 1
    return slot


def gather_steps(own_rows, observations, obs_mask, stages):
    parts = 1 << sum(len(stage) for stage in stages)

    def across(value, mask):
        return lax.ppermute(value, TIME_AXES, [(i, i ^ mask) for i in range(parts)])

    mask = 1 << stages[0][0]
    gathered = jnp.stack(
        [
            own_rows,
            jnp.concatenate(
                [across(observations, mask), across(obs_mask, mask).astype(jnp.float32)], 0
            ),
        ],
        0,
    )
    for stage in stages[1:]:
        masks = [1 << b for b in stage]
        if len(masks) == 2:
            masks = [masks[0] | masks[1], masks[1], masks[0]]
        arrived = []
        for m in masks:
            arrived.append(across(gathered, m))
        early = jnp.concatenate([gathered, arrived[0]], 0)
        gathered = jnp.concatenate([gathered] + arrived, 0)
    return early, gathered


def prepare(
    read_ref, mask_ref, map_ref, var_ref, trans_ref, noise_ref, mean_ref, prior_ref,
    start_ref, turned_ref, chosen_ref, inv_var_ref, trans_out, noise_out, mean_out, prior_out, rows_out,
):
    rows_out[...] = jnp.concatenate([read_ref[...], mask_ref[...].astype(jnp.float32)], 0)
    size = trans_ref.shape[0]
    sensors = map_ref.shape[1]
    trans = trans_ref[...]
    turned = trans.T
    turned_ref[...] = turned
    rows = jnp.concatenate(
        [trans * prior_ref[...], jnp.broadcast_to(mean_ref[...], (8, size))], 0
    )
    rows = dot3(rows, turned)
    start_ref[:size] = rows[:size] + noise_ref[...]
    start_ref[size:] = rows[size:]
    components = lax.broadcasted_iota(jnp.int32, (size, sensors), 0)
    chosen = (components == map_ref[...]).astype(jnp.float32)
    chosen_ref[...] = chosen.T.astype(jnp.bfloat16)
    inv_var_ref[...] = 1.0 / var_ref[...]
    trans_out[...] = trans
    noise_out[...] = noise_ref[...]
    mean_out[...] = mean_ref[...]
    prior_out[...] = prior_ref[...]


def kernel(
    steps_ref, start_ref, turned_ref, chosen_ref, inv_var_ref, trans_ref, noise_ref,
    mean_ref, prior_ref, tested_ref, mean_out, cov_out, prec_ref, info_ref, state_ref, check_ref,
    high_ref, low_ref, *, stages, known, early,
):
    rows_each = steps_ref.shape[1]
    parts = 1 << sum(len(stage) for stage in stages)
    per_part = rows_each // 2
    steps = parts * per_part
    size = trans_ref.shape[0]
    own = lax.axis_index("outer") * lax.axis_size("inner") + lax.axis_index("inner")
    first = own * per_part
    row_ids = lax.broadcasted_iota(jnp.int32, (size, size), 0)
    col_ids = lax.broadcasted_iota(jnp.int32, (size, size), 1)
    on_diag = row_ids == col_ids

    inv_var = inv_var_ref[...]

    head_slot = slot_of(own, stages)
    has_head = jnp.logical_and(head_slot < known, own > 0)
    headway = jnp.where(has_head, per_part, 0)

    def place(source, carried):
        if early:
            block = steps_ref[jnp.where(has_head, head_slot, 0)]
        else:
            block = steps_ref[slot_of(source ^ own, stages)]
        weight = block[per_part:] * inv_var
        prec_ref[pl.ds(source * per_part, per_part), :] = weight
        info_ref[pl.ds(source * per_part, per_part), :] = weight * block[:per_part]
        return carried

    if early:
        prec_ref[...] = jnp.zeros_like(prec_ref)
        info_ref[...] = jnp.zeros_like(info_ref)
        place(0, 0)
    else:
        lax.fori_loop(0, parts, place, 0, unroll=parts <= 8)
    chosen = chosen_ref[...]
    left = jnp.concatenate([prec_ref[...], info_ref[...]], 0)
    summed = jnp.zeros(left.shape, jnp.float32)
    for _ in range(3):
        part = left.astype(jnp.bfloat16)
        left = left - part.astype(jnp.float32)
        summed = summed + jnp.dot(part, chosen, preferred_element_type=jnp.float32)
    prec_ref[...] = summed[:steps]
    info_ref[...] = summed[steps:]
    high_ref[...], low_ref[...] = split(turned_ref[...])
    check_ref[...] = jnp.zeros_like(check_ref)
    if not early:
        check_ref[:per_part] = tested_ref[...]

    def factors(cov, mean, step):
        prec = prec_ref[pl.ds(step, 1), :]
        info = info_ref[pl.ds(step, 1), :]
        own_var = jnp.sum(jnp.where(on_diag, cov, 0.0), axis=0, keepdims=True)
        shrink = 1.0 / (1.0 + own_var * prec)
        series = jnp.where(on_diag, 0.0, cov * (prec * shrink))
        push = (info - prec * mean) * shrink
        return shrink, series, push

    square, wide, narrow = series_factors()
    whole = 1.0 / (square * wide[1] * narrow[1])

    def advance(cov, mean, step, move, outs):
        shrink, series, push = factors(cov, mean, step)
        whole_series = series
        series = split(series)
        lefts = []
        rights = []
        if move:
            lefts.append(trans_ref[...] * (shrink * whole))
            moved = mul(split(jnp.concatenate([cov, mean], 0)), (high_ref[...], low_ref[...]))
            rights.append(moved[:size])
        if outs:
            lefts.append(jnp.where(on_diag, jnp.broadcast_to(shrink * whole, (size, size)), 0.0))
            rights.append(cov)
        lefts[-1] = jnp.concatenate([lefts[-1], push * whole], 0)
        stacked = mul(split(jnp.concatenate([whole_series] + lefts, 0)), series)
        pow2 = stacked[:size]
        lowered = [stacked[size:]]
        if len(lefts) == 2:
            lowered = [stacked[size : 2 * size], stacked[2 * size :]]
        lefts = [left - low for left, low in zip(lefts, lowered)]
        pow2_split = split(pow2)
        pow4 = jnp.dot(pow2_split[0], pow2_split[0], preferred_element_type=jnp.float32)
        check_ref[step] = jnp.sum((pow4 * pow4).reshape(size // 8, 8, size), axis=0)
        even_left = split(pow4 + pow2 * wide[0])
        even_right = split(pow4 + pow2 * narrow[0])
        done = []
        for left in lefts:
            left = left * square + mul(split(left), pow2_split)
            done.append(split(left * wide[1] + mul(split(left), even_left)))
        rights = [split(right * narrow[1] + mul(even_right, split(right))) for right in rights]
        result = []
        if move:
            final = mul(done[0], rights[0])
            mean_next = final[size:] if not outs else mul(tuple(x[size:] for x in done[1]), rights[0])
            result += [final[:size] + noise_ref[...], mean_next + moved[size:]]
        if outs:
            final = mul(done[-1], rights[-1])
            result += [final[:size], final[size:] + mean]
        return result

    cov, mean = start_ref[:size], start_ref[size:]

    def body(step, carried):
        return tuple(advance(*carried, step, True, False))

    if early:
        cov, mean = lax.fori_loop(0, headway, body, (cov, mean))
        mean_out[:size] = cov
        mean_out[size:] = mean
        cov_out[...] = check_ref[:per_part]
        return
    cov, mean = lax.fori_loop(headway, first, body, (cov, mean))
    for j in range(per_part):
        moves = j + 1 < per_part
        result = advance(cov, mean, first + j, moves, True)
        if moves:
            cov, mean = result[:2]
        filt_cov, filt_mean = result[-2:]
        cov_out[j] = 0.5 * (filt_cov + filt_cov.T)
        mean_out[pl.ds(j, 1), :] = filt_mean[:1]

    sizes = jnp.sum(jnp.sum(check_ref[...], axis=1), axis=1, keepdims=True)
    failed = jnp.sum(jnp.where(sizes <= SERIES_BOUND, 0.0, 1.0))

    @pl.when(failed > 0.0)
    def _():
        lane = lax.broadcasted_iota(jnp.int32, (1, size), 1)

        def absorb(step, mean):
            prec = prec_ref[pl.ds(step, 1), :]
            info = info_ref[pl.ds(step, 1), :]

            def one(s, mean):
                here = lane == s

                def at(row):
                    return jnp.sum(jnp.where(here, row, 0.0), axis=1, keepdims=True)

                cov = state_ref[...]
                row = state_ref[pl.ds(s, 1), :]
                col = jnp.sum(jnp.where(here, cov, 0.0), axis=1, keepdims=True)
                scale = 1.0 / (1.0 + at(prec) * at(row))
                state_ref[...] = cov - col * (row * (at(prec) * scale))
                return mean + row * ((at(info) - at(prec) * at(mean)) * scale)

            mean = lax.fori_loop(0, size, one, mean)
            cov = state_ref[...]
            state_ref[...] = 0.5 * (cov + cov.T)
            return mean

        def predict(mean):
            cov = dot_full(dot_full(trans_ref[...], state_ref[...]), turned_ref[...])
            state_ref[...] = cov + noise_ref[...]
            return dot_full(jnp.broadcast_to(mean, (8, size)), turned_ref[...])[:1]

        state_ref[...] = dot_full(trans_ref[...] * prior_ref[...], turned_ref[...]) + noise_ref[...]
        mean = dot_full(jnp.broadcast_to(mean_ref[...], (8, size)), turned_ref[...])[:1]
        mean = lax.fori_loop(0, first, lambda t, m: predict(absorb(t, m)), mean)
        for j in range(per_part):
            mean = absorb(first + j, mean)
            cov_out[j] = state_ref[...]
            mean_out[pl.ds(j, 1), :] = mean
            if j + 1 < per_part:
                mean = predict(mean)


def local(
    observations, obs_mask, sensor_map, transition, proc_noise, obs_var, prior_mean, prior_var
):
    steps_here, sensors = observations.shape
    size = transition.shape[0]
    parts = lax.axis_size("outer") * lax.axis_size("inner")
    stages = exchange_stages(lax.axis_size("outer"), lax.axis_size("inner"))
    steps = parts * steps_here
    vmem = pl.BlockSpec(memory_space=pltpu.VMEM)

    def near(*arrays):
        return [pltpu.with_memory_space_constraint(a, pltpu.VMEM) for a in arrays]

    *prepared, own_rows = pl.pallas_call(
        prepare,
        out_shape=(
            pltpu.VMEM((size + 8, size), jnp.float32),
            pltpu.VMEM((size, size), jnp.float32),
            pltpu.VMEM((sensors, size), jnp.bfloat16),
            pltpu.VMEM((1, sensors), jnp.float32),
            pltpu.VMEM((size, size), jnp.float32),
            pltpu.VMEM((size, size), jnp.float32),
            pltpu.VMEM((1, size), jnp.float32),
            pltpu.VMEM((1, size), jnp.float32),
            pltpu.VMEM((2 * steps_here, sensors), jnp.float32),
        ),
        in_specs=[vmem] * 8,
        out_specs=(vmem,) * 9,
        name="prepare_window",
    )(
        observations, obs_mask, sensor_map[None], obs_var[None], transition, proc_noise,
        prior_mean[None], prior_var[None],
    )
    early, gathered = gather_steps(own_rows, observations, obs_mask, stages)
    scratch = [
        pltpu.VMEM((steps, sensors), jnp.float32),
        pltpu.VMEM((steps, sensors), jnp.float32),
        pltpu.VMEM((size, size), jnp.float32),
        pltpu.VMEM((steps, 8, size), jnp.float32),
        pltpu.VMEM((size, size), jnp.bfloat16),
        pltpu.VMEM((size, size), jnp.bfloat16),
    ]
    known = early.shape[0]
    untested = pltpu.VMEM((steps_here, 8, size), jnp.float32)

    def head(*refs):
        kernel(*refs[:9], None, *refs[9:], stages=stages, known=known, early=True)

    state, tested = pl.pallas_call(
        head,
        out_shape=(pltpu.VMEM((size + 8, size), jnp.float32), untested),
        in_specs=[vmem] * 9,
        out_specs=(vmem, vmem),
        scratch_shapes=scratch,
        name="filter_head",
    )(*near(early, *prepared))
    return pl.pallas_call(
        functools.partial(kernel, stages=stages, known=known, early=False),
        out_shape=(
            jax.ShapeDtypeStruct((steps_here, size), jnp.float32),
            jax.ShapeDtypeStruct((steps_here, size, size), jnp.float32),
        ),
        in_specs=[vmem] * 10,
        out_specs=(vmem, vmem),
        scratch_shapes=scratch,
        name="filter_window",
    )(*near(gathered, state, *prepared[1:], tested))


def solution(mesh):
    return jax.shard_map(
        local,
        mesh=mesh,
        in_specs=(
            P(("region", "outer", "inner"), None),
            P(("region", "outer", "inner"), None),
            P("region"),
            P(),
            P(),
            P(),
            P("region"),
            P("region"),
        ),
        out_specs=(
            P(("region", "outer", "inner"), None),
            P(("region", "outer", "inner"), None, None),
        ),
        check_vma=False,
    )
```
